512 devices in a mesh: rows: 128 (over z, x, y_lo), cols: 4 (over y_hi, core).
Axes of the slice: x: 4, y: 4 (y_hi: 2, y_lo: 2; y = y_hi * 2 + y_lo), z: 16, core: 2. Of those that a mesh axis runs over, the one named last changes fastest.
Arguments:
- events: float32 [32768, 16384], P('rows', 'cols'), may hold values from -520 to 520
- sample_mask: int32 [32768, 128], P('rows', 'cols'), may hold values from 0 to 1, as said below
- keep_rate: float32 [128], P('cols'), may hold values from 0.25 to 1, as said below
Outputs:
- similarity: float32 [256, 16384], P('rows', 'cols')
The draws below stay inside these ranges and needn't reach their ends.
Inputs may be any that keep to these rules, and one draw needn't show every extreme that they name: `sample_mask`: each entry is 1 with probability keep_rate of its block, independently of all others. `keep_rate`: multiples of 1/1024.
All inputs are finite; a program needn't handle non-finite values.
Results may differ from the reference program's by a relative error of at most 0.0001.
Values sent between devices are 32-bit elements; how exact they have to be, the bound alone decides.
No kernel may reach another device: no remote copies, remote signals or barrier semaphores. Data moves between devices by JAX's collectives and lax.ppermute only.
A program may use at most 64 MiB of HBM per device.

```python
import math
import jax
import jax.numpy as jnp
from jax import lax

COLUMNS = 16384
ROW_DEV = 256
QUERY_GROUP = 64
QUERIES = 256
MASK_BLOCKS = 128
ROWS = 32768
N_ROWS = 128
N_COLS = 4


def rate_levels(key):
    return jax.random.randint(jax.random.fold_in(key, 11), (MASK_BLOCKS,), 256, 1025)


def draw_keep_rate(key, part):
    return rate_levels(key).astype(jnp.float32) / 1024.0


def draw_sample_mask(key, part):
    levels = rate_levels(key)
    tickets = jax.random.randint(jax.random.fold_in(key, 12), (ROWS, MASK_BLOCKS), 0, 1024)
    return (tickets < levels[None, :]).astype(jnp.int32)


def draw_events(key, part):
    position = jnp.arange(ROWS, dtype=jnp.float32)
    rising = 1.0 + 2.0 * position / ROWS
    values = jnp.clip(jax.random.normal(jax.random.fold_in(key, 24), (ROWS, COLUMNS), jnp.float32), -6.0, 6.0)
    values = values * rising[:, None]
    return values.astype(jnp.float32)


def setup_inputs(seed: int = 0) -> dict:
    key_of = jax.random.split(jax.random.key(seed), 4)
    events = draw_events(jax.random.fold_in(key_of[3], 71), 0)
    sample_mask = draw_sample_mask(jax.random.fold_in(key_of[3], 71), 0)
    keep_rate = draw_keep_rate(jax.random.fold_in(key_of[3], 71), 0)
    return {"events": events, "sample_mask": sample_mask, "keep_rate": keep_rate}


def reference(events, sample_mask, keep_rate):
    span = COLUMNS // N_COLS
    order = jnp.arange(QUERIES, dtype=jnp.int32)
    source = (order // QUERY_GROUP * span + order % QUERY_GROUP).astype(jnp.int32)
    rates = jnp.repeat(keep_rate, 128)
    slabs = events.reshape(N_ROWS, ROW_DEV, COLUMNS)
    masks = sample_mask.reshape(N_ROWS, ROW_DEV, MASK_BLOCKS)

    def step(carry, inputs):
        gram, squares = carry
        slab, mask = inputs
        keep = jnp.repeat(mask, 128, axis=1).astype(slab.dtype)
        sampled = slab * keep
        picked = jnp.take(sampled, source, axis=1)
        gram = gram + lax.dot_general(picked, sampled, (((0,), (0,)), ((), ())), precision=lax.Precision.HIGHEST, preferred_element_type=gram.dtype)
        squares = squares + lax.optimization_barrier(jnp.sum(slab * slab, axis=0))
        return ((gram, squares), None)
    start = (jnp.zeros((QUERIES, COLUMNS), events.dtype), jnp.zeros((COLUMNS,), events.dtype))
    (gram, squares), _ = lax.scan(step, start, (slabs, masks))
    weight = lax.rsqrt(squares * rates + 1e-06)
    return math.sqrt(ROWS) * jnp.take(weight, source)[:, None] * gram * weight[None, :]
```

```python
import functools
import math

import jax
import jax.numpy as jnp
from jax import lax
from jax.experimental import pallas as pl
from jax.experimental.pallas import tpu as pltpu
from jax.sharding import Mesh
from jax.sharding import PartitionSpec as P

QUERY_GROUP = 64
BLOCK = 128
Z, X, Y = "rows_0", "rows_1", "rows_2"
ROWS = (Z, X, Y)
PLANE = (X, Y)
EPSILON = 1e-06
CHUNKS = 4


def split(values):
    high = values.astype(jnp.bfloat16)
    low = (values - high.astype(jnp.float32)).astype(jnp.bfloat16)
    return high, low


def gram_kernel(arrived, mask, events, gram, squares, high, low):
    groups, _, rows = arrived.shape
    plane, width = gram.shape[0], events.shape[1]
    step = pl.program_id(0)
    total_blocks = CHUNKS * (width // BLOCK)
    per_group = QUERY_GROUP // plane

    @pl.when(step == 0)
    def _():
        for group in range(groups):
            keep = arrived[group, QUERY_GROUP : QUERY_GROUP + 1, :]
            for place in range(plane):
                part = arrived[group, place * per_group : (place + 1) * per_group, :] * keep
                first = place * groups * per_group + group * per_group
                h, l = split(part)
                high[first : first + per_group, :] = h.astype(jnp.float32)
                low[first : first + per_group, :] = l.astype(jnp.float32)

    values = events[...]
    squares[...] = jnp.sum(values * values, axis=0, keepdims=True)
    blocks = width // BLOCK
    keep = mask[...].astype(jnp.float32)
    keep = jnp.concatenate([keep, jnp.zeros((BLOCK - blocks, rows), jnp.float32)], axis=0).T
    query_high = high[...].astype(jnp.bfloat16)
    query_low = low[...].astype(jnp.bfloat16)
    queries = groups * QUERY_GROUP
    each = queries // plane
    pair = 2 * BLOCK
    for start in range(0, width, pair):
        parts = []
        for at in range(start, start + pair, BLOCK):
            b = at // BLOCK
            parts.append(values[:, at : at + BLOCK] * keep[:, b : b + 1])
        h, l = split(jnp.concatenate(parts, axis=1))
        dot = functools.partial(jnp.dot, preferred_element_type=jnp.float32)
        result = dot(query_high, h) + (dot(query_high, l) + dot(query_low, h))
        for place in range(plane):
            for at in range(0, pair, BLOCK):
                block = step * blocks + (start + at) // BLOCK
                gram[place, pl.ds(block, each, stride=total_blocks), :] = result[
                    place * each : (place + 1) * each, at : at + BLOCK
                ]


def local_gram(arrived, mask, events, plane):
    groups, _, rows = arrived.shape
    queries = groups * QUERY_GROUP
    columns = events.shape[1]
    width = columns // CHUNKS
    shape = (plane, queries // plane * (columns // BLOCK), BLOCK)
    return pl.pallas_call(
        gram_kernel,
        grid=(CHUNKS,),
        in_specs=[
            pl.BlockSpec(arrived.shape, lambda i: (0, 0, 0)),
            pl.BlockSpec((width // BLOCK, rows), lambda i: (i, 0)),
            pl.BlockSpec((rows, width), lambda i: (0, i)),
        ],
        out_specs=[
            pl.BlockSpec(shape, lambda i: (0, 0, 0)),
            pl.BlockSpec((1, width), lambda i: (0, i)),
        ],
        out_shape=[
            jax.ShapeDtypeStruct(shape, jnp.float32),
            jax.ShapeDtypeStruct((1, columns), jnp.float32),
        ],
        scratch_shapes=[pltpu.VMEM((queries, rows), jnp.float32)] * 2,
        compiler_params=pltpu.CompilerParams(
            dimension_semantics=("arbitrary",), vmem_limit_bytes=40 << 20
        ),
        cost_estimate=pl.CostEstimate(
            flops=6 * queries * rows * columns,
            bytes_accessed=4 * (rows * columns + queries * columns),
            transcendentals=0,
        ),
        name="gram",
    )(arrived, mask, events)


def sent_to_all(shard, axis):
    copies = jnp.broadcast_to(shard, (lax.axis_size(axis), *shard.shape))
    return lax.all_to_all(copies, axis, split_axis=0, concat_axis=0, tiled=True)


def summed_by_pairs(value, axis):
    size, apart = lax.axis_size(axis), 1
    while apart < size:
        value = value + lax.ppermute(value, axis, [(i, i ^ apart) for i in range(size)])
        apart *= 2
    return value


def shards(events, sample_mask, keep_rate):
    rows, columns = events.shape
    depth, plane = lax.axis_size(Z), lax.axis_size(X) * lax.axis_size(Y)
    groups = lax.axis_size("cols")
    queries = groups * QUERY_GROUP
    share = queries // (depth * plane)

    mine = events[:, :QUERY_GROUP].reshape(rows, depth // groups, plane, share)
    mine = mine.transpose(2, 1, 3, 0).reshape(QUERY_GROUP, rows)
    keep = sample_mask[:, :1].astype(jnp.float32).T
    rate = jnp.broadcast_to(keep_rate[0], (1, rows))
    extra = jnp.concatenate([keep, rate, jnp.zeros((6, rows), jnp.float32)], axis=0)
    arrived = sent_to_all(jnp.concatenate([mine, extra], axis=0)[None], "cols")
    arrived = arrived.reshape(groups, QUERY_GROUP + 8, rows)

    gram, squares = local_gram(arrived, sample_mask.T, events, plane)
    raw = arrived[:, :QUERY_GROUP].reshape(groups, plane, -1, rows)
    query_squares = jnp.sum(raw * raw, axis=3).transpose(1, 0, 2).reshape(queries)
    query_rate = arrived[:, QUERY_GROUP + 1, 0]

    nearer = lax.all_to_all(gram, PLANE, split_axis=0, concat_axis=0, tiled=True)
    packed = jnp.concatenate([squares.reshape(-1, BLOCK), query_squares.reshape(-1, BLOCK)])
    for axis in (Y, X, Z):
        packed = summed_by_pairs(packed, axis)
    nearer, packed = lax.optimization_barrier((nearer, packed))
    nearer = nearer.sum(axis=0).reshape(depth, share * (columns // BLOCK), BLOCK)
    packed = packed.reshape(1, columns + queries)
    column_squares, query_squares = packed[:, :columns], packed[0, columns:]

    total = lax.all_to_all(nearer, Z, split_axis=0, concat_axis=0, tiled=True).sum(axis=0)
    total = total.reshape(share, columns)

    z, place = lax.axis_index(Z), lax.axis_index(PLANE)
    owned = lax.dynamic_slice_in_dim(query_squares, place * (queries // plane) + z * share, share)
    query_weight = lax.rsqrt(owned * query_rate[z // (depth // groups)] + EPSILON)
    rates = jnp.broadcast_to(keep_rate[:, None], (columns // BLOCK, BLOCK)).reshape(1, columns)
    column_weight = lax.rsqrt(column_squares * rates + EPSILON)
    factor = math.sqrt(rows * depth * plane)
    return factor * query_weight[:, None] * total * column_weight


def solution(mesh):
    torus = Mesh(mesh.devices.reshape(16, 4, 2, mesh.shape["cols"]), (Z, X, Y, "cols"))
    return jax.shard_map(
        shards,
        mesh=torus,
        in_specs=(P(ROWS, "cols"), P(ROWS, "cols"), P("cols")),
        out_specs=P(ROWS, "cols"),
        check_vma=False,
    )
```

```python
import functools
import math

import jax
import jax.numpy as jnp
from jax import lax
from jax.experimental import pallas as pl
from jax.experimental.pallas import tpu as pltpu
from jax.sharding import Mesh
from jax.sharding import PartitionSpec as P

QUERY_GROUP = 64
BLOCK = 128
ROWS = ("z", "x", "y")
ALL = ("z", "x", "y", "cols")
DEPTH, WIDTH, PAIR, GROUPS = 16, 4, 2, 4
FAN = 4
FAR = DEPTH // 2
QUERIES = GROUPS * QUERY_GROUP
EXTRA = 40
EPSILON = 1e-06
CHUNKS = 4


def device(z, x, y, c):
    return ((z * WIDTH + x) * PAIR + y) * GROUPS + c


def along_x():
    return {
        c: [
            [device(z, x, y, c) for x in range(WIDTH)]
            for z in range(DEPTH)
            for y in range(PAIR)
        ]
        for c in range(GROUPS)
    }


def along_pairs():
    return {
        c: [
            [device(2 * far + odd, x, y, c) for y in range(PAIR) for odd in range(2)]
            for far in range(FAR)
            for x in range(WIDTH)
        ]
        for c in range(GROUPS)
    }


def stages():
    x, pairs = along_x(), along_pairs()
    first = [g for c in range(GROUPS) for g in (pairs if c % 2 else x)[c]]
    second = [g for c in range(GROUPS) for g in (x if c % 2 else pairs)[c]]
    third = [
        [device(2 * far + odd, x, y, c) for far in range(FAR)]
        for odd in range(2)
        for x in range(WIDTH)
        for y in range(PAIR)
        for c in range(GROUPS)
    ]
    return first, second, third


def split(values):
    high = values.astype(jnp.bfloat16)
    low = (values - high.astype(jnp.float32)).astype(jnp.bfloat16)
    return high, low


def turned(left, right):
    return lax.dot_general(
        left,
        right,
        (((1,), (1,)), ((), ())),
        precision=lax.Precision.HIGHEST,
        preferred_element_type=jnp.float32,
    )


def query_kernel(mask, events, rate, sent):
    rows = events.shape[0]
    n = lax.broadcasted_iota(jnp.int32, (QUERY_GROUP, BLOCK), 0)
    column = lax.broadcasted_iota(jnp.int32, (QUERY_GROUP, BLOCK), 1)
    bit = [(n >> k) & 1 for k in range(6)]
    x_first = bit[1] * 32 + bit[2] * 16 + (n >> 4) * 4 + bit[3] * 2 + bit[0]
    y_first = bit[1] * 32 + bit[4] * 16 + ((n >> 2) & 3) * 4 + bit[5] * 2 + bit[0]
    values = events[...]
    for core, source in enumerate((x_first, y_first)):
        pick = (column == source).astype(jnp.float32)
        mine = turned(pick, values)
        for c in range(core, GROUPS, 2):
            sent[c, :QUERY_GROUP, :] = mine
    keep = mask[:1, :].astype(jnp.float32)
    scale = jnp.broadcast_to(rate[:, :1], (1, rows))
    last = jnp.concatenate([keep, scale, jnp.zeros((6, rows), jnp.float32)], axis=0)
    for c in range(GROUPS):
        sent[c, QUERY_GROUP:, :] = last


def own_queries(mask, events, rate):
    rows = events.shape[0]
    shape = (GROUPS, QUERY_GROUP + 8, rows)
    return pl.pallas_call(
        query_kernel,
        grid=(1,),
        in_specs=[
            pl.BlockSpec((8, rows), lambda i: (0, 0)),
            pl.BlockSpec((rows, BLOCK), lambda i: (0, 0)),
            pl.BlockSpec(rate.shape, lambda i: (0, 0)),
        ],
        out_specs=pl.BlockSpec(shape, lambda i: (0, 0, 0)),
        out_shape=jax.ShapeDtypeStruct(shape, jnp.float32),
        compiler_params=pltpu.CompilerParams(vmem_limit_bytes=60 << 20),
        cost_estimate=pl.CostEstimate(flops=1 << 25, bytes_accessed=1 << 19, transcendentals=0),
        name="queries",
    )(mask, events, rate)


def gram_kernel(arrived, mask, events, gram, high, low):
    rows, width = events.shape
    step = pl.program_id(0)
    blocks = width // BLOCK
    total_blocks = CHUNKS * blocks
    each = QUERIES // FAN
    squares_at = each * total_blocks
    run = QUERY_GROUP // (FAN * FAN)

    @pl.when(step == 0)
    def _():
        raw = []
        for place in range(FAN * FAN):
            parts = []
            for group in range(GROUPS):
                parts.append(arrived[group, place * run : (place + 1) * run, :])
            raw.append(jnp.concatenate(parts, axis=0))
            keeps = [
                jnp.broadcast_to(arrived[group, QUERY_GROUP : QUERY_GROUP + 1, :], (run, rows))
                for group in range(GROUPS)
            ]
            h, l = split(raw[-1] * jnp.concatenate(keeps, axis=0))
            first = place * run * GROUPS
            high[first : first + run * GROUPS, :] = h
            low[first : first + run * GROUPS, :] = l
        raw = jnp.concatenate(raw, axis=0)
        sums = turned(jnp.ones((8, rows), jnp.float32), raw * raw)[:1]
        last = jnp.concatenate([sums[:, k : k + BLOCK] for k in range(0, QUERIES, BLOCK)], axis=0)
        pad = EXTRA - total_blocks - QUERIES // BLOCK
        last = jnp.concatenate([last, jnp.zeros((pad, BLOCK), jnp.float32)], axis=0)
        for place in range(FAN):
            gram[place, squares_at + total_blocks :, :] = last

    values = events[...]
    squares = jnp.sum(values * values, axis=0, keepdims=True)
    for b in range(blocks):
        for place in range(FAN):
            gram[place, pl.ds(squares_at + step * blocks + b, 1), :] = squares[
                :, b * BLOCK : (b + 1) * BLOCK
            ]
    keep = mask[...].astype(jnp.float32)
    keep = jnp.concatenate([keep, jnp.zeros((BLOCK - blocks, rows), jnp.float32)], axis=0).T
    query_high, query_low = high[...], low[...]
    pair = 2 * BLOCK
    for start in range(0, width, pair):
        parts = []
        for at in range(start, start + pair, BLOCK):
            b = at // BLOCK
            parts.append(values[:, at : at + BLOCK] * keep[:, b : b + 1])
        h, l = split(jnp.concatenate(parts, axis=1))
        dot = functools.partial(jnp.dot, preferred_element_type=jnp.float32)
        result = dot(query_high, h) + (dot(query_high, l) + dot(query_low, h))
        for place in range(FAN):
            for at in range(0, pair, BLOCK):
                block = step * blocks + (start + at) // BLOCK
                gram[place, pl.ds(block, each, stride=total_blocks), :] = result[
                    place * each : (place + 1) * each, at : at + BLOCK
                ]


def local_gram(arrived, mask, events):
    rows, columns = events.shape
    width = columns // CHUNKS
    shape = (FAN, QUERIES // FAN * (columns // BLOCK) + EXTRA, BLOCK)
    return pl.pallas_call(
        gram_kernel,
        grid=(CHUNKS,),
        in_specs=[
            pl.BlockSpec(arrived.shape, lambda i: (0, 0, 0)),
            pl.BlockSpec((width // BLOCK, rows), lambda i: (i, 0)),
            pl.BlockSpec((rows, width), lambda i: (0, i)),
        ],
        out_specs=pl.BlockSpec(shape, lambda i: (0, 0, 0)),
        out_shape=jax.ShapeDtypeStruct(shape, jnp.float32),
        scratch_shapes=[pltpu.VMEM((QUERIES, rows), jnp.bfloat16)] * 2,
        compiler_params=pltpu.CompilerParams(
            dimension_semantics=("arbitrary",), vmem_limit_bytes=60 << 20
        ),
        cost_estimate=pl.CostEstimate(
            flops=6 * QUERIES * rows * columns,
            bytes_accessed=4 * (rows * columns + QUERIES * columns),
            transcendentals=0,
        ),
        name="gram",
    )(arrived, mask, events)


def exchanged(parts, groups):
    return lax.all_to_all(
        parts, ALL, split_axis=0, concat_axis=0, tiled=True, axis_index_groups=groups
    )


def parted(value, count):
    main, extra = value[:-EXTRA], value[-EXTRA:]
    main = main.reshape(count, -1, BLOCK)
    extra = jnp.broadcast_to(extra, (count, *extra.shape))
    return jnp.concatenate([main, extra], axis=1)


def shards(events, sample_mask, keep_rate):
    rows, columns = events.shape
    first, second, third = stages()
    share = QUERIES // (FAN * FAN * FAR)
    mask = sample_mask.T

    sent = own_queries(mask, events, keep_rate[None])
    arrived = lax.all_to_all(sent, "cols", split_axis=0, concat_axis=0, tiled=True)
    query_rate = arrived[:, QUERY_GROUP + 1, 0]

    total = exchanged(local_gram(arrived, mask, events), first).sum(axis=0)
    total = exchanged(parted(total, FAN), second).sum(axis=0)
    total = exchanged(parted(total, FAR), third).sum(axis=0)
    gram = total[:-EXTRA].reshape(share, columns)
    blocks = columns // BLOCK
    column_squares = total[-EXTRA : blocks - EXTRA].reshape(1, columns)
    query_squares = total[blocks - EXTRA : blocks - EXTRA + QUERIES // BLOCK].reshape(QUERIES)

    z, x, y, c = (lax.axis_index(a) for a in ALL)
    pairs = y * 2 + z % 2
    place = jnp.where(c % 2 == 0, x * FAN + pairs, pairs * FAN + x)
    owned = lax.dynamic_slice_in_dim(query_squares, place * (FAR * share) + z // 2 * share, share)
    owner_rate = lax.dynamic_slice_in_dim(query_rate, z // (DEPTH // GROUPS), 1)
    query_weight = lax.rsqrt(owned * owner_rate + EPSILON)
    rates = jnp.broadcast_to(keep_rate[:, None], (blocks, BLOCK)).reshape(1, columns)
    column_weight = lax.rsqrt(column_squares * rates + EPSILON)
    factor = math.sqrt(rows * DEPTH * WIDTH * PAIR)
    return factor * query_weight[:, None] * gram * column_weight


def solution(mesh):
    torus = Mesh(mesh.devices.reshape(DEPTH, WIDTH, PAIR, GROUPS), ALL)
    return jax.shard_map(
        shards,
        mesh=torus,
        in_specs=(P(ROWS, "cols"), P(ROWS, "cols"), P("cols")),
        out_specs=P(ROWS, "cols"),
        check_vma=False,
    )
```

```python
import functools
import math

import jax
import jax.numpy as jnp
from jax import lax
from jax.experimental import pallas as pl
from jax.experimental.pallas import tpu as pltpu
from jax.sharding import Mesh
from jax.sharding import PartitionSpec as P

QUERY_GROUP = 64
BLOCK = 128
ROWS = ("z", "x", "y")
ALL = ("z", "x", "y", "cols")
DEPTH, WIDTH, PAIR, GROUPS = 16, 4, 2, 4
FAN = 4
FAR = DEPTH // 2
QUERIES = GROUPS * QUERY_GROUP
EXTRA = 40
EPSILON = 1e-06
CHUNKS = 8


def device(z, x, y, c):
    return ((z * WIDTH + x) * PAIR + y) * GROUPS + c


def along_x():
    return {
        c: [
            [device(z, x, y, c) for x in range(WIDTH)]
            for z in range(DEPTH)
            for y in range(PAIR)
        ]
        for c in range(GROUPS)
    }


def along_pairs():
    return {
        c: [
            [device(2 * far + odd, x, y, c) for y in range(PAIR) for odd in range(2)]
            for far in range(FAR)
            for x in range(WIDTH)
        ]
        for c in range(GROUPS)
    }


def stages():
    x, pairs = along_x(), along_pairs()
    first = [g for c in range(GROUPS) for g in (pairs if c % 2 else x)[c]]
    second = [g for c in range(GROUPS) for g in (x if c % 2 else pairs)[c]]
    third = [
        [device(2 * far + odd, x, y, c) for far in range(FAR)]
        for odd in range(2)
        for x in range(WIDTH)
        for y in range(PAIR)
        for c in range(GROUPS)
    ]
    return first, second, third


def split(values):
    high = values.astype(jnp.bfloat16)
    low = (values - high.astype(jnp.float32)).astype(jnp.bfloat16)
    return high, low


def turned(left, right):
    return lax.dot_general(
        left,
        right,
        (((1,), (1,)), ((), ())),
        precision=lax.Precision.HIGHEST,
        preferred_element_type=jnp.float32,
    )


def query_kernel(mask, events, rate, sent):
    rows = events.shape[0]
    n = lax.broadcasted_iota(jnp.int32, (QUERY_GROUP, BLOCK), 0)
    column = lax.broadcasted_iota(jnp.int32, (QUERY_GROUP, BLOCK), 1)
    x, y, low, next_, query = n >> 4, (n >> 3) & 1, (n >> 2) & 1, (n >> 1) & 1, n & 1
    source = (next_ * 2 + low) * 16 + x * 4 + y * 2 + query
    sent[:QUERY_GROUP, :] = turned((column == source).astype(jnp.float32), events[...])
    keep = mask[:1, :].astype(jnp.float32)
    scale = jnp.broadcast_to(rate[:, :1], (1, rows))
    sent[QUERY_GROUP:, :] = jnp.concatenate(
        [keep, scale, jnp.zeros((6, rows), jnp.float32)], axis=0
    )


def own_queries(mask, events, rate):
    rows = events.shape[0]
    shape = (QUERY_GROUP + 8, rows)
    return pl.pallas_call(
        query_kernel,
        grid=(1,),
        in_specs=[
            pl.BlockSpec((8, rows), lambda i: (0, 0)),
            pl.BlockSpec((rows, BLOCK), lambda i: (0, 0)),
            pl.BlockSpec(rate.shape, lambda i: (0, 0)),
        ],
        out_specs=pl.BlockSpec(shape, lambda i: (0, 0)),
        out_shape=jax.ShapeDtypeStruct(shape, jnp.float32),
        compiler_params=pltpu.CompilerParams(vmem_limit_bytes=60 << 20),
        cost_estimate=pl.CostEstimate(flops=1 << 24, bytes_accessed=1 << 18, transcendentals=0),
        name="queries",
    )(mask, events, rate)


def gram_kernel(arrived, mask, events, gram, values, result, high, low, come, gone):
    rows, columns = events.shape
    width = columns // CHUNKS
    blocks = columns // BLOCK
    each = QUERIES // FAN
    extra_at = each * blocks
    run = QUERY_GROUP // (FAN * FAN)

    def incoming(k):
        part = pl.ds(k * width, width)
        return pltpu.make_async_copy(events.at[:, part], values.at[:, part], come.at[k])

    def outgoing(k):
        size = each * width // BLOCK
        part = pl.ds(k * size, size if k < CHUNKS else EXTRA)
        return pltpu.make_async_copy(result.at[:, part], gram.at[:, part], gone.at[k])

    for k in range(CHUNKS):
        incoming(k).start()

    core = lax.axis_index("cols") % 2
    raw = []
    for place in range(FAN * FAN):
        parts, keeps = [], []
        for group in range(GROUPS):
            parts.append(arrived[group, place * run : (place + 1) * run, :])
            keep = arrived[group, QUERY_GROUP : QUERY_GROUP + 1, :]
            keeps.append(jnp.broadcast_to(keep, (run, rows)))
        raw.append(jnp.concatenate(parts, axis=0))
        h, l = split(raw[-1] * jnp.concatenate(keeps, axis=0))
        at = jnp.where(core == 0, place, place % FAN * FAN + place // FAN)
        at = pl.multiple_of(at * (run * GROUPS), run * GROUPS)
        high[pl.ds(at, run * GROUPS), :] = h
        low[pl.ds(at, run * GROUPS), :] = l
    raw = jnp.concatenate(raw, axis=0)
    sums = turned(jnp.ones((8, rows), jnp.float32), raw * raw)[:1]
    last = [sums[:, k : k + BLOCK] for k in range(0, QUERIES, BLOCK)]
    last.append(jnp.zeros((EXTRA - blocks - len(last), BLOCK), jnp.float32))
    last = jnp.concatenate(last, axis=0)
    for place in range(FAN):
        result[place, extra_at + blocks :, :] = last

    keep = mask[...].astype(jnp.float32)
    keep = jnp.concatenate([keep, jnp.zeros((BLOCK - blocks, rows), jnp.float32)], axis=0).T
    query_high, query_low = high[...], low[...]
    dot = functools.partial(jnp.dot, preferred_element_type=jnp.float32)
    pair = 2 * BLOCK
    for k in range(CHUNKS):
        incoming(k).wait()
        for start in range(k * width, (k + 1) * width, pair):
            parts, squares = [], []
            for at in range(start, start + pair, BLOCK):
                b = at // BLOCK
                value = values[:, at : at + BLOCK]
                squares.append(jnp.sum(value * value, axis=0, keepdims=True))
                parts.append(value * keep[:, b : b + 1])
            h, l = split(jnp.concatenate(parts, axis=1))
            product = dot(query_high, h) + (dot(query_high, l) + dot(query_low, h))
            for place in range(FAN):
                for at in range(0, pair, BLOCK):
                    b = (start + at) // BLOCK
                    result[place, b * each : (b + 1) * each, :] = product[
                        place * each : (place + 1) * each, at : at + BLOCK
                    ]
                    result[place, extra_at + b : extra_at + b + 1, :] = squares[at // BLOCK]
        outgoing(k).start()
    outgoing(CHUNKS).start()
    for k in range(CHUNKS + 1):
        outgoing(k).wait()


def local_gram(arrived, mask, events):
    rows, columns = events.shape
    shape = (FAN, QUERIES // FAN * (columns // BLOCK) + EXTRA, BLOCK)
    whole = pl.BlockSpec(memory_space=pltpu.VMEM)
    there = pl.BlockSpec(memory_space=pl.ANY)
    return pl.pallas_call(
        gram_kernel,
        in_specs=[whole, whole, there],
        out_specs=there,
        out_shape=jax.ShapeDtypeStruct(shape, jnp.float32),
        scratch_shapes=[
            pltpu.VMEM(events.shape, jnp.float32),
            pltpu.VMEM(shape, jnp.float32),
            pltpu.VMEM((QUERIES, rows), jnp.bfloat16),
            pltpu.VMEM((QUERIES, rows), jnp.bfloat16),
            pltpu.SemaphoreType.DMA((CHUNKS,)),
            pltpu.SemaphoreType.DMA((CHUNKS + 1,)),
        ],
        compiler_params=pltpu.CompilerParams(vmem_limit_bytes=60 << 20),
        cost_estimate=pl.CostEstimate(
            flops=6 * QUERIES * rows * columns,
            bytes_accessed=4 * (rows * columns + QUERIES * columns),
            transcendentals=0,
        ),
        name="gram",
    )(arrived, mask, events)


def exchanged(parts, groups):
    return lax.all_to_all(
        parts, ALL, split_axis=0, concat_axis=0, tiled=True, axis_index_groups=groups
    )


def first_sum_kernel(arrived, total):
    rows = arrived.shape[1] - EXTRA
    each = QUERIES // FAN
    part = each // FAN

    def summed(at, size):
        whole = arrived[0, at : at + size, :]
        for sender in range(1, FAN):
            whole += arrived[sender, at : at + size, :]
        return whole

    for at in range(0, rows, each):
        whole = summed(at, each)
        for place in range(FAN):
            first = at // FAN
            total[place, first : first + part, :] = whole[place * part : (place + 1) * part]
    extra = summed(rows, EXTRA)
    for place in range(FAN):
        total[place, rows // FAN :, :] = extra


def first_sum(arrived):
    shape = (FAN, (arrived.shape[1] - EXTRA) // FAN + EXTRA, BLOCK)
    return pl.pallas_call(
        first_sum_kernel,
        out_shape=jax.ShapeDtypeStruct(shape, jnp.float32),
        compiler_params=pltpu.CompilerParams(vmem_limit_bytes=32 << 20),
        cost_estimate=pl.CostEstimate(
            flops=arrived.size, bytes_accessed=5 * arrived.size, transcendentals=0
        ),
        name="first_sum",
    )(arrived)


def second_sum_kernel(arrived, total, whole):
    rows = arrived.shape[1] - EXTRA
    value = arrived[0]
    for sender in range(1, FAN):
        value += arrived[sender]
    whole[...] = value
    each = QUERIES // (FAN * FAN)
    share = each // FAR
    blocks = rows // each
    for place in range(FAR):
        for query in range(share):
            total[place, query * blocks : (query + 1) * blocks, :] = whole[
                pl.ds(place * share + query, blocks, stride=each), :
            ]
        total[place, share * blocks :, :] = value[rows:]


def second_sum(arrived):
    shape = (FAR, (arrived.shape[1] - EXTRA) // FAR + EXTRA, BLOCK)
    return pl.pallas_call(
        second_sum_kernel,
        out_shape=jax.ShapeDtypeStruct(shape, jnp.float32),
        scratch_shapes=[pltpu.VMEM(arrived.shape[1:], jnp.float32)],
        compiler_params=pltpu.CompilerParams(vmem_limit_bytes=32 << 20),
        cost_estimate=pl.CostEstimate(
            flops=arrived.size, bytes_accessed=5 * arrived.size, transcendentals=0
        ),
        name="second_sum",
    )(arrived)


def last_sum_kernel(factor, arrived, queries, rates, similarity):
    total = arrived[0]
    for sender in range(1, FAR):
        total += arrived[sender]
    share, columns = similarity.shape
    blocks = columns // BLOCK
    squares = total[share * blocks : (share + 1) * blocks]
    weight = lax.rsqrt(squares * rates[...] + EPSILON) * factor

    z, x, y = (lax.axis_index(a) for a in ROWS)
    mine = ((x * FAN + y * 2 + z % 2) * FAR + z // 2) * share
    group = z // (DEPTH // GROUPS)
    query_squares = total[(share + 1) * blocks : (share + 1) * blocks + QUERIES // BLOCK]
    row = lax.broadcasted_iota(jnp.int32, query_squares.shape, 0)
    lane = lax.broadcasted_iota(jnp.int32, query_squares.shape, 1)
    query_rate = queries[0, 1:2, :1]
    for k in range(1, GROUPS):
        query_rate = jnp.where(group == k, queries[k, 1:2, :1], query_rate)
    for query in range(share):
        found = jnp.where(row * BLOCK + lane == mine + query, query_squares, 0.0)
        found = jnp.sum(jnp.sum(found, axis=1, keepdims=True), axis=0, keepdims=True)
        scale = lax.rsqrt(found * query_rate + EPSILON)
        result = total[query * blocks : (query + 1) * blocks] * weight * scale
        for b in range(blocks):
            similarity[query : query + 1, b * BLOCK : (b + 1) * BLOCK] = result[b : b + 1]


def last_sum(factor, arrived, queries, rates):
    blocks, share = rates.shape[0], QUERIES // (FAN * FAN * FAR)
    shape = (share, blocks * BLOCK)
    whole = lambda a: pl.BlockSpec(a.shape, lambda i: (0,) * a.ndim)
    return pl.pallas_call(
        functools.partial(last_sum_kernel, factor),
        grid=(1,),
        in_specs=[
            whole(arrived),
            pl.BlockSpec((GROUPS, 8, queries.shape[2]), lambda i: (0, QUERY_GROUP // 8, 0)),
            whole(rates),
        ],
        out_specs=pl.BlockSpec(shape, lambda i: (0, 0)),
        out_shape=jax.ShapeDtypeStruct(shape, jnp.float32),
        compiler_params=pltpu.CompilerParams(vmem_limit_bytes=32 << 20),
        cost_estimate=pl.CostEstimate(
            flops=arrived.size, bytes_accessed=5 * arrived.size, transcendentals=0
        ),
        name="last_sum",
    )(arrived, queries, rates)


def shards(events, sample_mask, keep_rate):
    first, second, third = stages()
    mask = sample_mask.T
    arrived = lax.all_gather(own_queries(mask, events, keep_rate[None]), "cols")
    total = first_sum(exchanged(local_gram(arrived, mask, events), first))
    total = second_sum(exchanged(total, second))
    factor = math.sqrt(events.shape[0] * DEPTH * WIDTH * PAIR)
    rates = jnp.broadcast_to(keep_rate[:, None], (keep_rate.size, BLOCK))
    return last_sum(factor, exchanged(total, third), arrived, rates)


def solution(mesh):
    torus = Mesh(mesh.devices.reshape(DEPTH, WIDTH, PAIR, GROUPS), ALL)
    return jax.shard_map(
        shards,
        mesh=torus,
        in_specs=(P(ROWS, "cols"), P(ROWS, "cols"), P("cols")),
        out_specs=P(ROWS, "cols"),
        check_vma=False,
    )
```

```python
import functools
import math

import jax
import jax.numpy as jnp
from jax import lax
from jax.experimental import pallas as pl
from jax.experimental.pallas import tpu as pltpu
from jax.sharding import Mesh
from jax.sharding import PartitionSpec as P

QUERY_GROUP = 64
BLOCK = 128
ROWS = ("z", "x", "y")
ALL = ("z", "x", "y", "cols")
DEPTH, WIDTH, PAIR, GROUPS = 16, 4, 2, 4
FAN = 4
FAR = DEPTH // 2
QUERIES = GROUPS * QUERY_GROUP
EXTRA = 40
EPSILON = 1e-06


def device(z, x, y, c):
    return ((z * WIDTH + x) * PAIR + y) * GROUPS + c


def along_x():
    return {
        c: [
            [device(z, x, y, c) for x in range(WIDTH)]
            for z in range(DEPTH)
            for y in range(PAIR)
        ]
        for c in range(GROUPS)
    }


def along_pairs():
    return {
        c: [
            [device(2 * far + odd, x, y, c) for y in range(PAIR) for odd in range(2)]
            for far in range(FAR)
            for x in range(WIDTH)
        ]
        for c in range(GROUPS)
    }


def stages():
    x, pairs = along_x(), along_pairs()
    first = [g for c in range(GROUPS) for g in (pairs if c % 2 else x)[c]]
    second = [g for c in range(GROUPS) for g in (x if c % 2 else pairs)[c]]
    third = [
        [device(2 * far + odd, x, y, c) for far in range(FAR)]
        for odd in range(2)
        for x in range(WIDTH)
        for y in range(PAIR)
        for c in range(GROUPS)
    ]
    return first, second, third


def split(values):
    high = values.astype(jnp.bfloat16)
    low = (values - high.astype(jnp.float32)).astype(jnp.bfloat16)
    return high, low


def turned(left, right):
    return lax.dot_general(
        left,
        right,
        (((1,), (1,)), ((), ())),
        precision=lax.Precision.HIGHEST,
        preferred_element_type=jnp.float32,
    )


def query_kernel(mask, near, rate, events, sent, held, come):
    incoming = pltpu.make_async_copy(events, held, come)
    incoming.start()
    rows = near.shape[0]
    n = lax.broadcasted_iota(jnp.int32, (QUERY_GROUP, BLOCK), 0)
    column = lax.broadcasted_iota(jnp.int32, (QUERY_GROUP, BLOCK), 1)
    x, y, low, next_, query = n >> 4, (n >> 3) & 1, (n >> 2) & 1, (n >> 1) & 1, n & 1
    source = (next_ * 2 + low) * 16 + x * 4 + y * 2 + query
    sent[:QUERY_GROUP, :] = turned((column == source).astype(jnp.float32), near[...])
    keep = mask[:1, :].astype(jnp.float32)
    scale = jnp.broadcast_to(rate[:, :1], (1, rows))
    sent[QUERY_GROUP:, :] = jnp.concatenate(
        [keep, scale, jnp.zeros((6, rows), jnp.float32)], axis=0
    )
    incoming.wait()


def own_queries(mask, events, rate):
    rows = events.shape[0]
    shape = (QUERY_GROUP + 8, rows)
    return pl.pallas_call(
        query_kernel,
        grid=(1,),
        in_specs=[
            pl.BlockSpec((8, rows), lambda i: (0, 0)),
            pl.BlockSpec((rows, BLOCK), lambda i: (0, 0)),
            pl.BlockSpec(rate.shape, lambda i: (0, 0)),
            pl.BlockSpec(memory_space=pl.ANY),
        ],
        out_specs=[
            pl.BlockSpec(shape, lambda i: (0, 0)),
            pl.BlockSpec(memory_space=pltpu.VMEM),
        ],
        out_shape=[
            jax.ShapeDtypeStruct(shape, jnp.float32),
            jax.ShapeDtypeStruct(events.shape, jnp.float32),
        ],
        scratch_shapes=[pltpu.SemaphoreType.DMA],
        compiler_params=pltpu.CompilerParams(vmem_limit_bytes=46 << 20),
        cost_estimate=pl.CostEstimate(flops=1 << 24, bytes_accessed=1 << 23, transcendentals=0),
        name="queries",
    )(mask, events, rate, events)


def gram_kernel(arrived, mask, values, result, high, low):
    rows, columns = values.shape
    blocks = columns // BLOCK
    each = QUERIES // FAN
    extra_at = each * blocks
    run = QUERY_GROUP // (FAN * FAN)

    core = lax.axis_index("cols") % 2
    raw = []
    for place in range(FAN * FAN):
        parts, keeps = [], []
        for group in range(GROUPS):
            parts.append(arrived[group, place * run : (place + 1) * run, :])
            keep = arrived[group, QUERY_GROUP : QUERY_GROUP + 1, :]
            keeps.append(jnp.broadcast_to(keep, (run, rows)))
        raw.append(jnp.concatenate(parts, axis=0))
        h, l = split(raw[-1] * jnp.concatenate(keeps, axis=0))
        at = jnp.where(core == 0, place, place % FAN * FAN + place // FAN)
        at = pl.multiple_of(at * (run * GROUPS), run * GROUPS)
        high[pl.ds(at, run * GROUPS), :] = h
        low[pl.ds(at, run * GROUPS), :] = l
    raw = jnp.concatenate(raw, axis=0)
    sums = turned(jnp.ones((8, rows), jnp.float32), raw * raw)[:1]
    last = [sums[:, k : k + BLOCK] for k in range(0, QUERIES, BLOCK)]
    last.append(jnp.zeros((EXTRA - blocks - len(last), BLOCK), jnp.float32))
    last = jnp.concatenate(last, axis=0)
    for place in range(FAN):
        result[place, extra_at + blocks :, :] = last

    keep = mask[...].astype(jnp.float32)
    keep = jnp.concatenate([keep, jnp.zeros((BLOCK - blocks, rows), jnp.float32)], axis=0).T
    query_high, query_low = high[...], low[...]
    query_all = jnp.concatenate([query_high, query_high, query_low], axis=1)
    dot = functools.partial(jnp.dot, preferred_element_type=jnp.float32)
    pair = 2 * BLOCK
    for start in range(0, columns, pair):
        parts = []
        for at in range(start, start + pair, BLOCK):
            b = at // BLOCK
            value = values[:, at : at + BLOCK]
            square = jnp.sum(value * value, axis=0, keepdims=True)
            for place in range(FAN):
                result[place, extra_at + b : extra_at + b + 1, :] = square
            parts.append(value * keep[:, b : b + 1])
        h, l = split(jnp.concatenate(parts, axis=1))
        product = dot(query_all, jnp.concatenate([h, l, h], axis=0))
        for place in range(FAN):
            for at in range(0, pair, BLOCK):
                b = (start + at) // BLOCK
                result[place, b * each : (b + 1) * each, :] = product[
                    place * each : (place + 1) * each, at : at + BLOCK
                ]


def local_gram(arrived, mask, events):
    rows, columns = events.shape
    shape = (FAN, QUERIES // FAN * (columns // BLOCK) + EXTRA, BLOCK)
    whole = pl.BlockSpec(memory_space=pltpu.VMEM)
    return pl.pallas_call(
        gram_kernel,
        in_specs=[whole, whole, whole],
        out_specs=whole,
        out_shape=jax.ShapeDtypeStruct(shape, jnp.float32),
        scratch_shapes=[
            pltpu.VMEM((QUERIES, rows), jnp.bfloat16),
            pltpu.VMEM((QUERIES, rows), jnp.bfloat16),
        ],
        compiler_params=pltpu.CompilerParams(vmem_limit_bytes=32 << 20),
        cost_estimate=pl.CostEstimate(
            flops=6 * QUERIES * rows * columns,
            bytes_accessed=4 * (rows * columns + QUERIES * columns),
            transcendentals=0,
        ),
        name="gram",
    )(arrived, mask, events)


def exchanged(parts, groups):
    return lax.all_to_all(
        parts, ALL, split_axis=0, concat_axis=0, tiled=True, axis_index_groups=groups
    )


def first_sum_kernel(arrived, total):
    rows = arrived.shape[1] - EXTRA
    each = QUERIES // FAN
    part = each // FAN

    def summed(at, size):
        whole = arrived[0, at : at + size, :]
        for sender in range(1, FAN):
            whole += arrived[sender, at : at + size, :]
        return whole

    for at in range(0, rows, each):
        whole = summed(at, each)
        for place in range(FAN):
            first = at // FAN
            total[place, first : first + part, :] = whole[place * part : (place + 1) * part]
    extra = summed(rows, EXTRA)
    for place in range(FAN):
        total[place, rows // FAN :, :] = extra


def first_sum(arrived):
    shape = (FAN, (arrived.shape[1] - EXTRA) // FAN + EXTRA, BLOCK)
    return pl.pallas_call(
        first_sum_kernel,
        out_shape=jax.ShapeDtypeStruct(shape, jnp.float32),
        compiler_params=pltpu.CompilerParams(vmem_limit_bytes=32 << 20),
        cost_estimate=pl.CostEstimate(
            flops=arrived.size, bytes_accessed=5 * arrived.size, transcendentals=0
        ),
        name="first_sum",
    )(arrived)


def second_sum_kernel(arrived, total, whole):
    rows = arrived.shape[1] - EXTRA
    value = arrived[0]
    for sender in range(1, FAN):
        value += arrived[sender]
    whole[...] = value
    each = QUERIES // (FAN * FAN)
    share = each // FAR
    blocks = rows // each
    for place in range(FAR):
        for query in range(share):
            total[place, query * blocks : (query + 1) * blocks, :] = whole[
                pl.ds(place * share + query, blocks, stride=each), :
            ]
        total[place, share * blocks :, :] = value[rows:]


def second_sum(arrived):
    shape = (FAR, (arrived.shape[1] - EXTRA) // FAR + EXTRA, BLOCK)
    return pl.pallas_call(
        second_sum_kernel,
        out_shape=jax.ShapeDtypeStruct(shape, jnp.float32),
        scratch_shapes=[pltpu.VMEM(arrived.shape[1:], jnp.float32)],
        compiler_params=pltpu.CompilerParams(vmem_limit_bytes=32 << 20),
        cost_estimate=pl.CostEstimate(
            flops=arrived.size, bytes_accessed=5 * arrived.size, transcendentals=0
        ),
        name="second_sum",
    )(arrived)


def last_sum_kernel(factor, arrived, queries, rates, similarity):
    total = arrived[0]
    for sender in range(1, FAR):
        total += arrived[sender]
    share, columns = similarity.shape
    blocks = columns // BLOCK
    squares = total[share * blocks : (share + 1) * blocks]
    weight = lax.rsqrt(squares * rates[...] + EPSILON) * factor

    z, x, y = (lax.axis_index(a) for a in ROWS)
    mine = ((x * FAN + y * 2 + z % 2) * FAR + z // 2) * share
    group = z // (DEPTH // GROUPS)
    query_squares = total[(share + 1) * blocks : (share + 1) * blocks + QUERIES // BLOCK]
    row = lax.broadcasted_iota(jnp.int32, query_squares.shape, 0)
    lane = lax.broadcasted_iota(jnp.int32, query_squares.shape, 1)
    query_rate = queries[0, 1:2, :1]
    for k in range(1, GROUPS):
        query_rate = jnp.where(group == k, queries[k, 1:2, :1], query_rate)
    for query in range(share):
        found = jnp.where(row * BLOCK + lane == mine + query, query_squares, 0.0)
        found = jnp.sum(jnp.sum(found, axis=1, keepdims=True), axis=0, keepdims=True)
        scale = lax.rsqrt(found * query_rate + EPSILON)
        result = total[query * blocks : (query + 1) * blocks] * weight * scale
        for b in range(blocks):
            similarity[query : query + 1, b * BLOCK : (b + 1) * BLOCK] = result[b : b + 1]


def last_sum(factor, arrived, queries, rates):
    blocks, share = rates.shape[0], QUERIES // (FAN * FAN * FAR)
    shape = (share, blocks * BLOCK)
    whole = lambda a: pl.BlockSpec(a.shape, lambda i: (0,) * a.ndim)
    return pl.pallas_call(
        functools.partial(last_sum_kernel, factor),
        grid=(1,),
        in_specs=[
            whole(arrived),
            pl.BlockSpec((GROUPS, 8, queries.shape[2]), lambda i: (0, QUERY_GROUP // 8, 0)),
            whole(rates),
        ],
        out_specs=pl.BlockSpec(shape, lambda i: (0, 0)),
        out_shape=jax.ShapeDtypeStruct(shape, jnp.float32),
        compiler_params=pltpu.CompilerParams(vmem_limit_bytes=32 << 20),
        cost_estimate=pl.CostEstimate(
            flops=arrived.size, bytes_accessed=5 * arrived.size, transcendentals=0
        ),
        name="last_sum",
    )(arrived, queries, rates)


def shards(events, sample_mask, keep_rate):
    first, second, third = stages()
    mask = sample_mask.T
    own, events = own_queries(mask, events, keep_rate[None])
    arrived = lax.all_gather(own, "cols")
    total = first_sum(exchanged(local_gram(arrived, mask, events), first))
    total = second_sum(exchanged(total, second))
    factor = math.sqrt(events.shape[0] * DEPTH * WIDTH * PAIR)
    rates = jnp.broadcast_to(keep_rate[:, None], (keep_rate.size, BLOCK))
    return last_sum(factor, exchanged(total, third), arrived, rates)


def solution(mesh):
    torus = Mesh(mesh.devices.reshape(DEPTH, WIDTH, PAIR, GROUPS), ALL)
    return jax.shard_map(
        shards,
        mesh=torus,
        in_specs=(P(ROWS, "cols"), P(ROWS, "cols"), P("cols")),
        out_specs=P(ROWS, "cols"),
        check_vma=False,
    )
```

```python
import functools
import math

import jax
import jax.numpy as jnp
from jax import lax
from jax.experimental import pallas as pl
from jax.experimental.pallas import tpu as pltpu
from jax.sharding import Mesh
from jax.sharding import PartitionSpec as P

QUERY_GROUP = 64
BLOCK = 128
ROWS = ("z", "x", "y")
ALL = ("z", "x", "y", "cols")
DEPTH, WIDTH, PAIR, GROUPS = 16, 4, 2, 4
FAN = 4
FAR = DEPTH // 2
QUERIES = GROUPS * QUERY_GROUP
EXTRA = 40
EPSILON = 1e-06


def device(z, x, y, c):
    return ((z * WIDTH + x) * PAIR + y) * GROUPS + c


def along_x():
    return {
        c: [
            [device(z, x, y, c) for x in range(WIDTH)]
            for z in range(DEPTH)
            for y in range(PAIR)
        ]
        for c in range(GROUPS)
    }


def along_pairs():
    return {
        c: [
            [device(2 * far + odd, x, y, c) for y in range(PAIR) for odd in range(2)]
            for far in range(FAR)
            for x in range(WIDTH)
        ]
        for c in range(GROUPS)
    }


def stages():
    x, pairs = along_x(), along_pairs()
    first = [g for c in range(GROUPS) for g in (pairs if c % 2 else x)[c]]
    second = [g for c in range(GROUPS) for g in (x if c % 2 else pairs)[c]]
    third = [
        [device(2 * far + odd, x, y, c) for far in range(FAR)]
        for odd in range(2)
        for x in range(WIDTH)
        for y in range(PAIR)
        for c in range(GROUPS)
    ]
    return first, second, third


def split(values):
    high = values.astype(jnp.bfloat16)
    low = (values - high.astype(jnp.float32)).astype(jnp.bfloat16)
    return high, low


def turned(left, right):
    return lax.dot_general(
        left,
        right,
        (((1,), (1,)), ((), ())),
        precision=lax.Precision.HIGHEST,
        preferred_element_type=jnp.float32,
    )


def query_kernel(mask, events, rate, sent):
    rows = events.shape[0]
    n = lax.broadcasted_iota(jnp.int32, (QUERY_GROUP, BLOCK), 0)
    column = lax.broadcasted_iota(jnp.int32, (QUERY_GROUP, BLOCK), 1)
    x, y, low, next_, query = n >> 4, (n >> 3) & 1, (n >> 2) & 1, (n >> 1) & 1, n & 1
    source = (next_ * 2 + low) * 16 + x * 4 + y * 2 + query
    sent[:QUERY_GROUP, :] = turned((column == source).astype(jnp.float32), events[...])
    keep = mask[:1, :].astype(jnp.float32)
    scale = jnp.broadcast_to(rate[:, :1], (1, rows))
    sent[QUERY_GROUP:, :] = jnp.concatenate(
        [keep, scale, jnp.zeros((6, rows), jnp.float32)], axis=0
    )


def own_queries(mask, events, rate):
    rows = events.shape[0]
    shape = (QUERY_GROUP + 8, rows)
    return pl.pallas_call(
        query_kernel,
        grid=(1,),
        in_specs=[
            pl.BlockSpec((8, rows), lambda i: (0, 0)),
            pl.BlockSpec((rows, BLOCK), lambda i: (0, 0)),
            pl.BlockSpec(rate.shape, lambda i: (0, 0)),
        ],
        out_specs=pl.BlockSpec(shape, lambda i: (0, 0)),
        out_shape=jax.ShapeDtypeStruct(shape, jnp.float32),
        compiler_params=pltpu.CompilerParams(vmem_limit_bytes=56 << 20),
        cost_estimate=pl.CostEstimate(flops=1 << 24, bytes_accessed=1 << 18, transcendentals=0),
        name="queries",
    )(mask, events, rate)


def gram_kernel(arrived, mask, values, result, high, low):
    rows, columns = values.shape
    blocks = columns // BLOCK
    each = QUERIES // FAN
    extra_at = each * blocks
    run = QUERY_GROUP // (FAN * FAN)

    core = lax.axis_index("cols") % 2
    raw = []
    for place in range(FAN * FAN):
        parts, keeps = [], []
        for group in range(GROUPS):
            parts.append(arrived[group, place * run : (place + 1) * run, :])
            keep = arrived[group, QUERY_GROUP : QUERY_GROUP + 1, :]
            keeps.append(jnp.broadcast_to(keep, (run, rows)))
        raw.append(jnp.concatenate(parts, axis=0))
        h, l = split(raw[-1] * jnp.concatenate(keeps, axis=0))
        at = jnp.where(core == 0, place, place % FAN * FAN + place // FAN)
        at = pl.multiple_of(at * (run * GROUPS), run * GROUPS)
        high[pl.ds(at, run * GROUPS), :] = h
        low[pl.ds(at, run * GROUPS), :] = l
    raw = jnp.concatenate(raw, axis=0)
    sums = turned(jnp.ones((8, rows), jnp.float32), raw * raw)[:1]
    last = [sums[:, k : k + BLOCK] for k in range(0, QUERIES, BLOCK)]
    last.append(jnp.zeros((EXTRA - blocks - len(last), BLOCK), jnp.float32))
    last = jnp.concatenate(last, axis=0)
    for place in range(FAN):
        result[place, extra_at + blocks :, :] = last

    keep = mask[...].astype(jnp.float32)
    keep = jnp.concatenate([keep, jnp.zeros((BLOCK - blocks, rows), jnp.float32)], axis=0).T
    query_high, query_low = high[...], low[...]
    query_all = jnp.concatenate([query_high, query_high, query_low], axis=1)
    dot = functools.partial(jnp.dot, preferred_element_type=jnp.float32)
    pair = 2 * BLOCK
    for start in range(0, columns, pair):
        parts = []
        for at in range(start, start + pair, BLOCK):
            b = at // BLOCK
            value = values[:, at : at + BLOCK]
            square = jnp.sum(value * value, axis=0, keepdims=True)
            for place in range(FAN):
                result[place, extra_at + b : extra_at + b + 1, :] = square
            parts.append(value * keep[:, b : b + 1])
        h, l = split(jnp.concatenate(parts, axis=1))
        product = dot(query_all, jnp.concatenate([h, l, h], axis=0))
        for place in range(FAN):
            for at in range(0, pair, BLOCK):
                b = (start + at) // BLOCK
                result[place, b * each : (b + 1) * each, :] = product[
                    place * each : (place + 1) * each, at : at + BLOCK
                ]


def local_gram(arrived, mask, events):
    rows, columns = events.shape
    shape = (FAN, QUERIES // FAN * (columns // BLOCK) + EXTRA, BLOCK)
    whole = pl.BlockSpec(memory_space=pltpu.VMEM)
    return pl.pallas_call(
        gram_kernel,
        in_specs=[whole, whole, whole],
        out_specs=whole,
        out_shape=jax.ShapeDtypeStruct(shape, jnp.float32),
        scratch_shapes=[
            pltpu.VMEM((QUERIES, rows), jnp.bfloat16),
            pltpu.VMEM((QUERIES, rows), jnp.bfloat16),
        ],
        compiler_params=pltpu.CompilerParams(vmem_limit_bytes=32 << 20),
        cost_estimate=pl.CostEstimate(
            flops=6 * QUERIES * rows * columns,
            bytes_accessed=4 * (rows * columns + QUERIES * columns),
            transcendentals=0,
        ),
        name="gram",
    )(arrived, mask, events)


def exchanged(parts, groups):
    return lax.all_to_all(
        parts, ALL, split_axis=0, concat_axis=0, tiled=True, axis_index_groups=groups
    )


def first_sum_kernel(arrived, total):
    rows = arrived.shape[1] - EXTRA
    each = QUERIES // FAN
    part = each // FAN

    def summed(at, size):
        whole = arrived[0, at : at + size, :]
        for sender in range(1, FAN):
            whole += arrived[sender, at : at + size, :]
        return whole

    for at in range(0, rows, each):
        whole = summed(at, each)
        for place in range(FAN):
            first = at // FAN
            total[place, first : first + part, :] = whole[place * part : (place + 1) * part]
    extra = summed(rows, EXTRA)
    for place in range(FAN):
        total[place, rows // FAN :, :] = extra


def first_sum(arrived):
    shape = (FAN, (arrived.shape[1] - EXTRA) // FAN + EXTRA, BLOCK)
    return pl.pallas_call(
        first_sum_kernel,
        out_shape=jax.ShapeDtypeStruct(shape, jnp.float32),
        compiler_params=pltpu.CompilerParams(vmem_limit_bytes=32 << 20),
        cost_estimate=pl.CostEstimate(
            flops=arrived.size, bytes_accessed=5 * arrived.size, transcendentals=0
        ),
        name="first_sum",
    )(arrived)


def second_sum_kernel(arrived, total, whole):
    rows = arrived.shape[1] - EXTRA
    value = arrived[0]
    for sender in range(1, FAN):
        value += arrived[sender]
    whole[...] = value
    each = QUERIES // (FAN * FAN)
    share = each // FAR
    blocks = rows // each
    for place in range(FAR):
        for query in range(share):
            total[place, query * blocks : (query + 1) * blocks, :] = whole[
                pl.ds(place * share + query, blocks, stride=each), :
            ]
        total[place, share * blocks :, :] = value[rows:]


def second_sum(arrived):
    shape = (FAR, (arrived.shape[1] - EXTRA) // FAR + EXTRA, BLOCK)
    return pl.pallas_call(
        second_sum_kernel,
        out_shape=jax.ShapeDtypeStruct(shape, jnp.float32),
        scratch_shapes=[pltpu.VMEM(arrived.shape[1:], jnp.float32)],
        compiler_params=pltpu.CompilerParams(vmem_limit_bytes=32 << 20),
        cost_estimate=pl.CostEstimate(
            flops=arrived.size, bytes_accessed=5 * arrived.size, transcendentals=0
        ),
        name="second_sum",
    )(arrived)


def last_sum_kernel(factor, arrived, queries, rates, similarity):
    total = arrived[0]
    for sender in range(1, FAR):
        total += arrived[sender]
    share, columns = similarity.shape
    blocks = columns // BLOCK
    squares = total[share * blocks : (share + 1) * blocks]
    weight = lax.rsqrt(squares * rates[...] + EPSILON) * factor

    z, x, y = (lax.axis_index(a) for a in ROWS)
    mine = ((x * FAN + y * 2 + z % 2) * FAR + z // 2) * share
    group = z // (DEPTH // GROUPS)
    query_squares = total[(share + 1) * blocks : (share + 1) * blocks + QUERIES // BLOCK]
    row = lax.broadcasted_iota(jnp.int32, query_squares.shape, 0)
    lane = lax.broadcasted_iota(jnp.int32, query_squares.shape, 1)
    query_rate = queries[0, 1:2, :1]
    for k in range(1, GROUPS):
        query_rate = jnp.where(group == k, queries[k, 1:2, :1], query_rate)
    for query in range(share):
        found = jnp.where(row * BLOCK + lane == mine + query, query_squares, 0.0)
        found = jnp.sum(jnp.sum(found, axis=1, keepdims=True), axis=0, keepdims=True)
        scale = lax.rsqrt(found * query_rate + EPSILON)
        result = total[query * blocks : (query + 1) * blocks] * weight * scale
        for b in range(blocks):
            similarity[query : query + 1, b * BLOCK : (b + 1) * BLOCK] = result[b : b + 1]


def last_sum(factor, arrived, queries, rates):
    blocks, share = rates.shape[0], QUERIES // (FAN * FAN * FAR)
    shape = (share, blocks * BLOCK)
    whole = lambda a: pl.BlockSpec(a.shape, lambda i: (0,) * a.ndim)
    return pl.pallas_call(
        functools.partial(last_sum_kernel, factor),
        grid=(1,),
        in_specs=[
            whole(arrived),
            pl.BlockSpec((GROUPS, 8, queries.shape[2]), lambda i: (0, QUERY_GROUP // 8, 0)),
            whole(rates),
        ],
        out_specs=pl.BlockSpec(shape, lambda i: (0, 0)),
        out_shape=jax.ShapeDtypeStruct(shape, jnp.float32),
        compiler_params=pltpu.CompilerParams(vmem_limit_bytes=32 << 20),
        cost_estimate=pl.CostEstimate(
            flops=arrived.size, bytes_accessed=5 * arrived.size, transcendentals=0
        ),
        name="last_sum",
    )(arrived, queries, rates)


def shards(events, sample_mask, keep_rate):
    first, second, third = stages()
    mask = sample_mask.T
    arrived = lax.all_gather(own_queries(mask, events, keep_rate[None]), "cols")
    total = first_sum(exchanged(local_gram(arrived, mask, events), first))
    total = second_sum(exchanged(total, second))
    factor = math.sqrt(events.shape[0] * DEPTH * WIDTH * PAIR)
    rates = jnp.broadcast_to(keep_rate[:, None], (keep_rate.size, BLOCK))
    return last_sum(factor, exchanged(total, third), arrived, rates)


def solution(mesh):
    torus = Mesh(mesh.devices.reshape(DEPTH, WIDTH, PAIR, GROUPS), ALL)
    return jax.shard_map(
        shards,
        mesh=torus,
        in_specs=(P(ROWS, "cols"), P(ROWS, "cols"), P("cols")),
        out_specs=P(ROWS, "cols"),
        check_vma=False,
    )
```

```python
import functools
import math

import jax
import jax.numpy as jnp
from jax import lax
from jax.experimental import pallas as pl
from jax.experimental.pallas import tpu as pltpu
from jax.sharding import Mesh
from jax.sharding import PartitionSpec as P

QUERY_GROUP = 64
BLOCK = 128
ROWS = ("z", "x", "y")
ALL = ("z", "x", "y", "cols")
DEPTH, WIDTH, PAIR, GROUPS = 16, 4, 2, 4
FAN = 4
FAR = DEPTH // 2
QUERIES = GROUPS * QUERY_GROUP
EXTRA = 40
EPSILON = 1e-06


def device(z, x, y, c):
    return ((z * WIDTH + x) * PAIR + y) * GROUPS + c


CORE_0_CLASSES = ((0, 3), (1, 2))
CORE_1_CLASSES = ((0, 1), (3, 2))


def block_of(core, x, y, odd):
    if core == 0:
        shared = next(k for k, places in enumerate(CORE_0_CLASSES) if x in places)
        return shared * 2 + odd, CORE_0_CLASSES[shared].index(x) * 2 + y
    shared = next(k for k, places in enumerate(CORE_1_CLASSES) if x in places)
    return shared * 2 + y, CORE_1_CLASSES[shared].index(x) * 2 + odd


def stages():
    first, second = [], []
    for c in range(0, GROUPS, 2):
        for pair in zip(*CORE_0_CLASSES):
            first += [
                [device((2 * far - odd) % DEPTH, x, y, c) for x in pair for odd in range(2)]
                for far in range(FAR)
                for y in range(PAIR)
            ]
        for shared in CORE_0_CLASSES:
            second += [
                [device(z, x, y, c) for x in shared for y in range(PAIR)] for z in range(DEPTH)
            ]
    for c in range(1, GROUPS, 2):
        for pair in zip(*CORE_1_CLASSES):
            first += [
                [device(z, x, y, c) for x in pair for y in range(PAIR)] for z in range(DEPTH)
            ]
        for shared in CORE_1_CLASSES:
            second += [
                [device(2 * far + odd, x, y, c) for x in shared for odd in range(2)]
                for far in range(FAR)
                for y in range(PAIR)
            ]
    third = [
        [device(2 * far + odd, x, y, c) for far in range(FAR)]
        for odd in range(2)
        for x in range(WIDTH)
        for y in range(PAIR)
        for c in range(GROUPS)
    ]
    return first, second, third


def split(values):
    high = values.astype(jnp.bfloat16)
    low = (values - high.astype(jnp.float32)).astype(jnp.bfloat16)
    return high, low


def turned(left, right):
    return lax.dot_general(
        left,
        right,
        (((1,), (1,)), ((), ())),
        precision=lax.Precision.HIGHEST,
        preferred_element_type=jnp.float32,
    )


def query_kernel(mask, events, rate, sent):
    rows = events.shape[0]
    n = lax.broadcasted_iota(jnp.int32, (QUERY_GROUP, BLOCK), 0)
    column = lax.broadcasted_iota(jnp.int32, (QUERY_GROUP, BLOCK), 1)
    x, y, low, next_, query = n >> 4, (n >> 3) & 1, (n >> 2) & 1, (n >> 1) & 1, n & 1
    source = (next_ * 2 + low) * 16 + x * 4 + y * 2 + query
    sent[:QUERY_GROUP, :] = turned((column == source).astype(jnp.float32), events[...])
    keep = mask[:1, :].astype(jnp.float32)
    scale = jnp.broadcast_to(rate[:, :1], (1, rows))
    sent[QUERY_GROUP:, :] = jnp.concatenate(
        [keep, scale, jnp.zeros((6, rows), jnp.float32)], axis=0
    )


def own_queries(mask, events, rate):
    rows = events.shape[0]
    shape = (QUERY_GROUP + 8, rows)
    return pl.pallas_call(
        query_kernel,
        grid=(1,),
        in_specs=[
            pl.BlockSpec((8, rows), lambda i: (0, 0)),
            pl.BlockSpec((rows, BLOCK), lambda i: (0, 0)),
            pl.BlockSpec(rate.shape, lambda i: (0, 0)),
        ],
        out_specs=pl.BlockSpec(shape, lambda i: (0, 0)),
        out_shape=jax.ShapeDtypeStruct(shape, jnp.float32),
        compiler_params=pltpu.CompilerParams(vmem_limit_bytes=56 << 20),
        cost_estimate=pl.CostEstimate(flops=1 << 24, bytes_accessed=1 << 18, transcendentals=0),
        name="queries",
    )(mask, events, rate)


def gram_kernel(arrived, mask, values, result, high, low):
    rows, columns = values.shape
    blocks = columns // BLOCK
    each = QUERIES // FAN
    extra_at = each * blocks
    run = QUERY_GROUP // (FAN * FAN)

    core = lax.axis_index("cols") % 2
    raw = []
    for place in range(FAN * FAN):
        parts, keeps = [], []
        for group in range(GROUPS):
            parts.append(arrived[group, place * run : (place + 1) * run, :])
            keep = arrived[group, QUERY_GROUP : QUERY_GROUP + 1, :]
            keeps.append(jnp.broadcast_to(keep, (run, rows)))
        raw.append(jnp.concatenate(parts, axis=0))
        h, l = split(raw[-1] * jnp.concatenate(keeps, axis=0))
        spots = []
        for each_core in range(2):
            near, far = block_of(each_core, place // FAN, place // 2 % 2, place % 2)
            spots.append(near * FAN + far)
        at = jnp.where(core == 0, *spots)
        at = pl.multiple_of(at * (run * GROUPS), run * GROUPS)
        high[pl.ds(at, run * GROUPS), :] = h
        low[pl.ds(at, run * GROUPS), :] = l
    raw = jnp.concatenate(raw, axis=0)
    sums = turned(jnp.ones((8, rows), jnp.float32), raw * raw)[:1]
    last = [sums[:, k : k + BLOCK] for k in range(0, QUERIES, BLOCK)]
    last.append(jnp.zeros((EXTRA - blocks - len(last), BLOCK), jnp.float32))
    last = jnp.concatenate(last, axis=0)
    for place in range(FAN):
        result[place, extra_at + blocks :, :] = last

    keep = mask[...].astype(jnp.float32)
    keep = jnp.concatenate([keep, jnp.zeros((BLOCK - blocks, rows), jnp.float32)], axis=0).T
    query_high, query_low = high[...], low[...]
    query_all = jnp.concatenate([query_high, query_high, query_low], axis=1)
    dot = functools.partial(jnp.dot, preferred_element_type=jnp.float32)
    pair = 2 * BLOCK
    for start in range(0, columns, pair):
        parts = []
        for at in range(start, start + pair, BLOCK):
            b = at // BLOCK
            value = values[:, at : at + BLOCK]
            square = jnp.sum(value * value, axis=0, keepdims=True)
            for place in range(FAN):
                result[place, extra_at + b : extra_at + b + 1, :] = square
            parts.append(value * keep[:, b : b + 1])
        h, l = split(jnp.concatenate(parts, axis=1))
        product = dot(query_all, jnp.concatenate([h, l, h], axis=0))
        for place in range(FAN):
            for at in range(0, pair, BLOCK):
                b = (start + at) // BLOCK
                result[place, b * each : (b + 1) * each, :] = product[
                    place * each : (place + 1) * each, at : at + BLOCK
                ]


def local_gram(arrived, mask, events):
    rows, columns = events.shape
    shape = (FAN, QUERIES // FAN * (columns // BLOCK) + EXTRA, BLOCK)
    whole = pl.BlockSpec(memory_space=pltpu.VMEM)
    return pl.pallas_call(
        gram_kernel,
        in_specs=[whole, whole, whole],
        out_specs=whole,
        out_shape=jax.ShapeDtypeStruct(shape, jnp.float32),
        scratch_shapes=[
            pltpu.VMEM((QUERIES, rows), jnp.bfloat16),
            pltpu.VMEM((QUERIES, rows), jnp.bfloat16),
        ],
        compiler_params=pltpu.CompilerParams(vmem_limit_bytes=32 << 20),
        cost_estimate=pl.CostEstimate(
            flops=6 * QUERIES * rows * columns,
            bytes_accessed=4 * (rows * columns + QUERIES * columns),
            transcendentals=0,
        ),
        name="gram",
    )(arrived, mask, events)


def exchanged(parts, groups):
    return lax.all_to_all(
        parts, ALL, split_axis=0, concat_axis=0, tiled=True, axis_index_groups=groups
    )


def first_sum_kernel(arrived, total):
    rows = arrived.shape[1] - EXTRA
    each = QUERIES // FAN
    part = each // FAN

    def summed(at, size):
        whole = arrived[0, at : at + size, :]
        for sender in range(1, FAN):
            whole += arrived[sender, at : at + size, :]
        return whole

    for at in range(0, rows, each):
        whole = summed(at, each)
        for place in range(FAN):
            first = at // FAN
            total[place, first : first + part, :] = whole[place * part : (place + 1) * part]
    extra = summed(rows, EXTRA)
    for place in range(FAN):
        total[place, rows // FAN :, :] = extra


def first_sum(arrived):
    shape = (FAN, (arrived.shape[1] - EXTRA) // FAN + EXTRA, BLOCK)
    return pl.pallas_call(
        first_sum_kernel,
        out_shape=jax.ShapeDtypeStruct(shape, jnp.float32),
        compiler_params=pltpu.CompilerParams(vmem_limit_bytes=32 << 20),
        cost_estimate=pl.CostEstimate(
            flops=arrived.size, bytes_accessed=5 * arrived.size, transcendentals=0
        ),
        name="first_sum",
    )(arrived)


def second_sum_kernel(arrived, total, whole):
    rows = arrived.shape[1] - EXTRA
    value = arrived[0]
    for sender in range(1, FAN):
        value += arrived[sender]
    whole[...] = value
    each = QUERIES // (FAN * FAN)
    share = each // FAR
    blocks = rows // each
    for place in range(FAR):
        for query in range(share):
            total[place, query * blocks : (query + 1) * blocks, :] = whole[
                pl.ds(place * share + query, blocks, stride=each), :
            ]
        total[place, share * blocks :, :] = value[rows:]


def second_sum(arrived):
    shape = (FAR, (arrived.shape[1] - EXTRA) // FAR + EXTRA, BLOCK)
    return pl.pallas_call(
        second_sum_kernel,
        out_shape=jax.ShapeDtypeStruct(shape, jnp.float32),
        scratch_shapes=[pltpu.VMEM(arrived.shape[1:], jnp.float32)],
        compiler_params=pltpu.CompilerParams(vmem_limit_bytes=32 << 20),
        cost_estimate=pl.CostEstimate(
            flops=arrived.size, bytes_accessed=5 * arrived.size, transcendentals=0
        ),
        name="second_sum",
    )(arrived)


def last_sum_kernel(factor, arrived, queries, rates, similarity):
    total = arrived[0]
    for sender in range(1, FAR):
        total += arrived[sender]
    share, columns = similarity.shape
    blocks = columns // BLOCK
    squares = total[share * blocks : (share + 1) * blocks]
    weight = lax.rsqrt(squares * rates[...] + EPSILON) * factor

    z, x, y = (lax.axis_index(a) for a in ROWS)
    mine = ((x * FAN + y * 2 + z % 2) * FAR + z // 2) * share
    group = z // (DEPTH // GROUPS)
    query_squares = total[(share + 1) * blocks : (share + 1) * blocks + QUERIES // BLOCK]
    row = lax.broadcasted_iota(jnp.int32, query_squares.shape, 0)
    lane = lax.broadcasted_iota(jnp.int32, query_squares.shape, 1)
    query_rate = queries[0, 1:2, :1]
    for k in range(1, GROUPS):
        query_rate = jnp.where(group == k, queries[k, 1:2, :1], query_rate)
    for query in range(share):
        found = jnp.where(row * BLOCK + lane == mine + query, query_squares, 0.0)
        found = jnp.sum(jnp.sum(found, axis=1, keepdims=True), axis=0, keepdims=True)
        scale = lax.rsqrt(found * query_rate + EPSILON)
        result = total[query * blocks : (query + 1) * blocks] * weight * scale
        for b in range(blocks):
            similarity[query : query + 1, b * BLOCK : (b + 1) * BLOCK] = result[b : b + 1]


def last_sum(factor, arrived, queries, rates):
    blocks, share = rates.shape[0], QUERIES // (FAN * FAN * FAR)
    shape = (share, blocks * BLOCK)
    whole = lambda a: pl.BlockSpec(a.shape, lambda i: (0,) * a.ndim)
    return pl.pallas_call(
        functools.partial(last_sum_kernel, factor),
        grid=(1,),
        in_specs=[
            whole(arrived),
            pl.BlockSpec((GROUPS, 8, queries.shape[2]), lambda i: (0, QUERY_GROUP // 8, 0)),
            whole(rates),
        ],
        out_specs=pl.BlockSpec(shape, lambda i: (0, 0)),
        out_shape=jax.ShapeDtypeStruct(shape, jnp.float32),
        compiler_params=pltpu.CompilerParams(vmem_limit_bytes=32 << 20),
        cost_estimate=pl.CostEstimate(
            flops=arrived.size, bytes_accessed=5 * arrived.size, transcendentals=0
        ),
        name="last_sum",
    )(arrived, queries, rates)


def shards(events, sample_mask, keep_rate):
    first, second, third = stages()
    mask = sample_mask.T
    arrived = lax.all_gather(own_queries(mask, events, keep_rate[None]), "cols")
    total = first_sum(exchanged(local_gram(arrived, mask, events), first))
    total = second_sum(exchanged(total, second))
    factor = math.sqrt(events.shape[0] * DEPTH * WIDTH * PAIR)
    rates = jnp.broadcast_to(keep_rate[:, None], (keep_rate.size, BLOCK))
    return last_sum(factor, exchanged(total, third), arrived, rates)


def solution(mesh):
    torus = Mesh(mesh.devices.reshape(DEPTH, WIDTH, PAIR, GROUPS), ALL)
    return jax.shard_map(
        shards,
        mesh=torus,
        in_specs=(P(ROWS, "cols"), P(ROWS, "cols"), P("cols")),
        out_specs=P(ROWS, "cols"),
        check_vma=False,
    )
```

```python
import functools
import math

import jax
import jax.numpy as jnp
from jax import lax
from jax.experimental import pallas as pl
from jax.experimental.pallas import tpu as pltpu
from jax.sharding import Mesh
from jax.sharding import PartitionSpec as P

QUERY_GROUP = 64
BLOCK = 128
ROWS = ("z", "x", "y")
ALL = ("z", "x", "y", "cols")
DEPTH, WIDTH, PAIR, GROUPS = 16, 4, 2, 4
FAN = 4
FAR = DEPTH // 2
QUERIES = GROUPS * QUERY_GROUP
EXTRA = 40
EPSILON = 1e-06


def device(z, x, y, c):
    return ((z * WIDTH + x) * PAIR + y) * GROUPS + c


CORE_0_CLASSES = ((0, 3), (1, 2))
CORE_1_CLASSES = ((0, 1), (3, 2))


def block_of(core, x, y, odd):
    if core == 0:
        shared = next(k for k, places in enumerate(CORE_0_CLASSES) if x in places)
        return shared * 2 + odd, CORE_0_CLASSES[shared].index(x) * 2 + y
    shared = next(k for k, places in enumerate(CORE_1_CLASSES) if x in places)
    return shared * 2 + y, CORE_1_CLASSES[shared].index(x) * 2 + odd


def stages():
    first, second = [], []
    for c in range(0, GROUPS, 2):
        for pair in zip(*CORE_0_CLASSES):
            first += [
                [device(2 * far + odd, x, y, c) for x in pair for odd in range(2)]
                for far in range(FAR)
                for y in range(PAIR)
            ]
        for shared in CORE_0_CLASSES:
            second += [
                [device(z, x, y, c) for x in shared for y in range(PAIR)] for z in range(DEPTH)
            ]
    for c in range(1, GROUPS, 2):
        for pair in zip(*CORE_1_CLASSES):
            first += [
                [device(z, x, y, c) for x in pair for y in range(PAIR)] for z in range(DEPTH)
            ]
        for shared in CORE_1_CLASSES:
            second += [
                [device(2 * far + odd, x, y, c) for x in shared for odd in range(2)]
                for far in range(FAR)
                for y in range(PAIR)
            ]
    third = [
        [device(2 * far + odd, x, y, c) for far in range(FAR)]
        for odd in range(2)
        for x in range(WIDTH)
        for y in range(PAIR)
        for c in range(GROUPS)
    ]
    return first, second, third


def split(values):
    high = values.astype(jnp.bfloat16)
    low = (values - high.astype(jnp.float32)).astype(jnp.bfloat16)
    return high, low


def turned(left, right):
    return lax.dot_general(
        left,
        right,
        (((1,), (1,)), ((), ())),
        precision=lax.Precision.HIGHEST,
        preferred_element_type=jnp.float32,
    )


def query_kernel(mask, events, rate, sent):
    rows = events.shape[0]
    n = lax.broadcasted_iota(jnp.int32, (QUERY_GROUP, BLOCK), 0)
    column = lax.broadcasted_iota(jnp.int32, (QUERY_GROUP, BLOCK), 1)
    x, y, low, next_, query = n >> 4, (n >> 3) & 1, (n >> 2) & 1, (n >> 1) & 1, n & 1
    source = (next_ * 2 + low) * 16 + x * 4 + y * 2 + query
    sent[:QUERY_GROUP, :] = turned((column == source).astype(jnp.float32), events[...])
    keep = mask[:1, :].astype(jnp.float32)
    scale = jnp.broadcast_to(rate[:, :1], (1, rows))
    sent[QUERY_GROUP:, :] = jnp.concatenate(
        [keep, scale, jnp.zeros((6, rows), jnp.float32)], axis=0
    )


def own_queries(mask, events, rate):
    rows = events.shape[0]
    shape = (QUERY_GROUP + 8, rows)
    return pl.pallas_call(
        query_kernel,
        grid=(1,),
        in_specs=[
            pl.BlockSpec((8, rows), lambda i: (0, 0)),
            pl.BlockSpec((rows, BLOCK), lambda i: (0, 0)),
            pl.BlockSpec(rate.shape, lambda i: (0, 0)),
        ],
        out_specs=pl.BlockSpec(shape, lambda i: (0, 0)),
        out_shape=jax.ShapeDtypeStruct(shape, jnp.float32),
        compiler_params=pltpu.CompilerParams(vmem_limit_bytes=56 << 20),
        cost_estimate=pl.CostEstimate(flops=1 << 24, bytes_accessed=1 << 18, transcendentals=0),
        name="queries",
    )(mask, events, rate)


def gram_kernel(arrived, mask, values, result, high, low):
    rows, columns = values.shape
    blocks = columns // BLOCK
    each = QUERIES // FAN
    extra_at = each * blocks
    run = QUERY_GROUP // (FAN * FAN)

    core = lax.axis_index("cols") % 2
    raw = []
    for place in range(FAN * FAN):
        parts, keeps = [], []
        for group in range(GROUPS):
            parts.append(arrived[group, place * run : (place + 1) * run, :])
            keep = arrived[group, QUERY_GROUP : QUERY_GROUP + 1, :]
            keeps.append(jnp.broadcast_to(keep, (run, rows)))
        raw.append(jnp.concatenate(parts, axis=0))
        h, l = split(raw[-1] * jnp.concatenate(keeps, axis=0))
        spots = []
        for each_core in range(2):
            near, far = block_of(each_core, place // FAN, place // 2 % 2, place % 2)
            spots.append(near * FAN + far)
        at = jnp.where(core == 0, *spots)
        at = pl.multiple_of(at * (run * GROUPS), run * GROUPS)
        high[pl.ds(at, run * GROUPS), :] = h
        low[pl.ds(at, run * GROUPS), :] = l
    raw = jnp.concatenate(raw, axis=0)
    sums = turned(jnp.ones((8, rows), jnp.float32), raw * raw)[:1]
    last = [sums[:, k : k + BLOCK] for k in range(0, QUERIES, BLOCK)]
    last.append(jnp.zeros((EXTRA - blocks - len(last), BLOCK), jnp.float32))
    last = jnp.concatenate(last, axis=0)
    for place in range(FAN):
        result[place, extra_at + blocks :, :] = last

    keep = mask[...].astype(jnp.float32)
    keep = jnp.concatenate([keep, jnp.zeros((BLOCK - blocks, rows), jnp.float32)], axis=0).T
    query_high, query_low = high[...], low[...]
    query_all = jnp.concatenate([query_high, query_high, query_low], axis=1)
    dot = functools.partial(jnp.dot, preferred_element_type=jnp.float32)
    pair = 2 * BLOCK
    for start in range(0, columns, pair):
        parts = []
        for at in range(start, start + pair, BLOCK):
            b = at // BLOCK
            value = values[:, at : at + BLOCK]
            square = jnp.sum(value * value, axis=0, keepdims=True)
            for place in range(FAN):
                result[place, extra_at + b : extra_at + b + 1, :] = square
            parts.append(value * keep[:, b : b + 1])
        h, l = split(jnp.concatenate(parts, axis=1))
        product = dot(query_all, jnp.concatenate([h, l, h], axis=0))
        for place in range(FAN):
            for at in range(0, pair, BLOCK):
                b = (start + at) // BLOCK
                result[place, b * each : (b + 1) * each, :] = product[
                    place * each : (place + 1) * each, at : at + BLOCK
                ]


def local_gram(arrived, mask, events):
    rows, columns = events.shape
    shape = (FAN, QUERIES // FAN * (columns // BLOCK) + EXTRA, BLOCK)
    whole = pl.BlockSpec(memory_space=pltpu.VMEM)
    return pl.pallas_call(
        gram_kernel,
        in_specs=[whole, whole, whole],
        out_specs=whole,
        out_shape=jax.ShapeDtypeStruct(shape, jnp.float32),
        scratch_shapes=[
            pltpu.VMEM((QUERIES, rows), jnp.bfloat16),
            pltpu.VMEM((QUERIES, rows), jnp.bfloat16),
        ],
        compiler_params=pltpu.CompilerParams(vmem_limit_bytes=32 << 20),
        cost_estimate=pl.CostEstimate(
            flops=6 * QUERIES * rows * columns,
            bytes_accessed=4 * (rows * columns + QUERIES * columns),
            transcendentals=0,
        ),
        name="gram",
    )(arrived, mask, events)


def exchanged(parts, groups):
    return lax.all_to_all(
        parts, ALL, split_axis=0, concat_axis=0, tiled=True, axis_index_groups=groups
    )


def first_sum_kernel(arrived, total):
    rows = arrived.shape[1] - EXTRA
    each = QUERIES // FAN
    part = each // FAN

    def summed(at, size):
        whole = arrived[0, at : at + size, :]
        for sender in range(1, FAN):
            whole += arrived[sender, at : at + size, :]
        return whole

    for at in range(0, rows, each):
        whole = summed(at, each)
        for place in range(FAN):
            first = at // FAN
            total[place, first : first + part, :] = whole[place * part : (place + 1) * part]
    extra = summed(rows, EXTRA)
    for place in range(FAN):
        total[place, rows // FAN :, :] = extra


def first_sum(arrived):
    shape = (FAN, (arrived.shape[1] - EXTRA) // FAN + EXTRA, BLOCK)
    return pl.pallas_call(
        first_sum_kernel,
        out_shape=jax.ShapeDtypeStruct(shape, jnp.float32),
        compiler_params=pltpu.CompilerParams(vmem_limit_bytes=32 << 20),
        cost_estimate=pl.CostEstimate(
            flops=arrived.size, bytes_accessed=5 * arrived.size, transcendentals=0
        ),
        name="first_sum",
    )(arrived)


def second_sum_kernel(arrived, total, whole):
    rows = arrived.shape[1] - EXTRA
    value = arrived[0]
    for sender in range(1, FAN):
        value += arrived[sender]
    whole[...] = value
    each = QUERIES // (FAN * FAN)
    share = each // FAR
    blocks = rows // each
    for place in range(FAR):
        for query in range(share):
            total[place, query * blocks : (query + 1) * blocks, :] = whole[
                pl.ds(place * share + query, blocks, stride=each), :
            ]
        total[place, share * blocks :, :] = value[rows:]


def second_sum(arrived):
    shape = (FAR, (arrived.shape[1] - EXTRA) // FAR + EXTRA, BLOCK)
    return pl.pallas_call(
        second_sum_kernel,
        out_shape=jax.ShapeDtypeStruct(shape, jnp.float32),
        scratch_shapes=[pltpu.VMEM(arrived.shape[1:], jnp.float32)],
        compiler_params=pltpu.CompilerParams(vmem_limit_bytes=32 << 20),
        cost_estimate=pl.CostEstimate(
            flops=arrived.size, bytes_accessed=5 * arrived.size, transcendentals=0
        ),
        name="second_sum",
    )(arrived)


def last_sum_kernel(factor, arrived, queries, rates, similarity):
    total = arrived[0]
    for sender in range(1, FAR):
        total += arrived[sender]
    share, columns = similarity.shape
    blocks = columns // BLOCK
    squares = total[share * blocks : (share + 1) * blocks]
    weight = lax.rsqrt(squares * rates[...] + EPSILON) * factor

    z, x, y = (lax.axis_index(a) for a in ROWS)
    mine = ((x * FAN + y * 2 + z % 2) * FAR + z // 2) * share
    group = z // (DEPTH // GROUPS)
    query_squares = total[(share + 1) * blocks : (share + 1) * blocks + QUERIES // BLOCK]
    row = lax.broadcasted_iota(jnp.int32, query_squares.shape, 0)
    lane = lax.broadcasted_iota(jnp.int32, query_squares.shape, 1)
    query_rate = queries[0, 1:2, :1]
    for k in range(1, GROUPS):
        query_rate = jnp.where(group == k, queries[k, 1:2, :1], query_rate)
    for query in range(share):
        found = jnp.where(row * BLOCK + lane == mine + query, query_squares, 0.0)
        found = jnp.sum(jnp.sum(found, axis=1, keepdims=True), axis=0, keepdims=True)
        scale = lax.rsqrt(found * query_rate + EPSILON)
        result = total[query * blocks : (query + 1) * blocks] * weight * scale
        for b in range(blocks):
            similarity[query : query + 1, b * BLOCK : (b + 1) * BLOCK] = result[b : b + 1]


def last_sum(factor, arrived, queries, rates):
    blocks, share = rates.shape[0], QUERIES // (FAN * FAN * FAR)
    shape = (share, blocks * BLOCK)
    whole = lambda a: pl.BlockSpec(a.shape, lambda i: (0,) * a.ndim)
    return pl.pallas_call(
        functools.partial(last_sum_kernel, factor),
        grid=(1,),
        in_specs=[
            whole(arrived),
            pl.BlockSpec((GROUPS, 8, queries.shape[2]), lambda i: (0, QUERY_GROUP // 8, 0)),
            whole(rates),
        ],
        out_specs=pl.BlockSpec(shape, lambda i: (0, 0)),
        out_shape=jax.ShapeDtypeStruct(shape, jnp.float32),
        compiler_params=pltpu.CompilerParams(vmem_limit_bytes=32 << 20),
        cost_estimate=pl.CostEstimate(
            flops=arrived.size, bytes_accessed=5 * arrived.size, transcendentals=0
        ),
        name="last_sum",
    )(arrived, queries, rates)


def shards(events, sample_mask, keep_rate):
    first, second, third = stages()
    mask = sample_mask.T
    arrived = lax.all_gather(own_queries(mask, events, keep_rate[None]), "cols")
    total = first_sum(exchanged(local_gram(arrived, mask, events), first))
    total = second_sum(exchanged(total, second))
    factor = math.sqrt(events.shape[0] * DEPTH * WIDTH * PAIR)
    rates = jnp.broadcast_to(keep_rate[:, None], (keep_rate.size, BLOCK))
    return last_sum(factor, exchanged(total, third), arrived, rates)


def solution(mesh):
    torus = Mesh(mesh.devices.reshape(DEPTH, WIDTH, PAIR, GROUPS), ALL)
    return jax.shard_map(
        shards,
        mesh=torus,
        in_specs=(P(ROWS, "cols"), P(ROWS, "cols"), P("cols")),
        out_specs=P(ROWS, "cols"),
        check_vma=False,
    )
```

```python
import functools
import math

import jax
import jax.numpy as jnp
from jax import lax
from jax.experimental import pallas as pl
from jax.experimental.pallas import tpu as pltpu
from jax.sharding import Mesh
from jax.sharding import PartitionSpec as P

QUERY_GROUP = 64
BLOCK = 128
ROWS = ("z", "x", "y")
ALL = ("z", "x", "y", "cols")
DEPTH, WIDTH, PAIR, GROUPS = 16, 4, 2, 4
FAN = 4
FAR = DEPTH // 2
QUERIES = GROUPS * QUERY_GROUP
EXTRA = 40
EPSILON = 1e-06


def device(z, x, y, c):
    return ((z * WIDTH + x) * PAIR + y) * GROUPS + c


def along_x():
    return {
        c: [
            [device(z, x, y, c) for x in range(WIDTH)]
            for z in range(DEPTH)
            for y in range(PAIR)
        ]
        for c in range(GROUPS)
    }


def along_pairs():
    return {
        c: [
            [device(2 * far + odd, x, y, c) for y in range(PAIR) for odd in range(2)]
            for far in range(FAR)
            for x in range(WIDTH)
        ]
        for c in range(GROUPS)
    }


def stages():
    x, pairs = along_x(), along_pairs()
    first = [g for c in range(GROUPS) for g in (pairs if c % 2 else x)[c]]
    second = [g for c in range(GROUPS) for g in (x if c % 2 else pairs)[c]]
    third = [
        [device(2 * far + odd, x, y, c) for far in range(FAR)]
        for odd in range(2)
        for x in range(WIDTH)
        for y in range(PAIR)
        for c in range(GROUPS)
    ]
    return first, second, third


def split(values):
    high = values.astype(jnp.bfloat16)
    low = (values - high.astype(jnp.float32)).astype(jnp.bfloat16)
    return high, low


def turned(left, right):
    return lax.dot_general(
        left,
        right,
        (((1,), (1,)), ((), ())),
        precision=lax.Precision.HIGHEST,
        preferred_element_type=jnp.float32,
    )


def query_kernel(mask, events, rate, sent):
    rows = events.shape[0]
    n = lax.broadcasted_iota(jnp.int32, (QUERY_GROUP, BLOCK), 0)
    column = lax.broadcasted_iota(jnp.int32, (QUERY_GROUP, BLOCK), 1)
    x, y, low, next_, query = n >> 4, (n >> 3) & 1, (n >> 2) & 1, (n >> 1) & 1, n & 1
    source = (next_ * 2 + low) * 16 + x * 4 + y * 2 + query
    sent[:QUERY_GROUP, :] = turned((column == source).astype(jnp.float32), events[...])
    keep = mask[:1, :].astype(jnp.float32)
    scale = jnp.broadcast_to(rate[:, :1], (1, rows))
    sent[QUERY_GROUP:, :] = jnp.concatenate(
        [keep, scale, jnp.zeros((6, rows), jnp.float32)], axis=0
    )


def own_queries(mask, events, rate):
    rows = events.shape[0]
    shape = (QUERY_GROUP + 8, rows)
    return pl.pallas_call(
        query_kernel,
        grid=(1,),
        in_specs=[
            pl.BlockSpec((8, rows), lambda i: (0, 0)),
            pl.BlockSpec((rows, BLOCK), lambda i: (0, 0)),
            pl.BlockSpec(rate.shape, lambda i: (0, 0)),
        ],
        out_specs=pl.BlockSpec(shape, lambda i: (0, 0)),
        out_shape=jax.ShapeDtypeStruct(shape, jnp.float32),
        compiler_params=pltpu.CompilerParams(vmem_limit_bytes=56 << 20),
        cost_estimate=pl.CostEstimate(flops=1 << 24, bytes_accessed=1 << 18, transcendentals=0),
        name="queries",
    )(mask, events, rate)


def gram_kernel(arrived, mask, values, result, high, low):
    rows, columns = values.shape
    blocks = columns // BLOCK
    each = QUERIES // FAN
    extra_at = each * blocks
    run = QUERY_GROUP // (FAN * FAN)

    core = lax.axis_index("cols") % 2
    raw = []
    for place in range(FAN * FAN):
        parts, keeps = [], []
        for group in range(GROUPS):
            parts.append(arrived[group, place * run : (place + 1) * run, :])
            keep = arrived[group, QUERY_GROUP : QUERY_GROUP + 1, :]
            keeps.append(jnp.broadcast_to(keep, (run, rows)))
        raw.append(jnp.concatenate(parts, axis=0))
        h, l = split(raw[-1] * jnp.concatenate(keeps, axis=0))
        at = jnp.where(core == 0, place, place % FAN * FAN + place // FAN)
        at = pl.multiple_of(at * (run * GROUPS), run * GROUPS)
        high[pl.ds(at, run * GROUPS), :] = h
        low[pl.ds(at, run * GROUPS), :] = l
    raw = jnp.concatenate(raw, axis=0)
    sums = turned(jnp.ones((8, rows), jnp.float32), raw * raw)[:1]
    last = [sums[:, k : k + BLOCK] for k in range(0, QUERIES, BLOCK)]
    last.append(jnp.zeros((EXTRA - blocks - len(last), BLOCK), jnp.float32))
    last = jnp.concatenate(last, axis=0)
    for place in range(FAN):
        result[place, extra_at + blocks :, :] = last

    keep = mask[...].astype(jnp.float32)
    keep = jnp.concatenate([keep, jnp.zeros((BLOCK - blocks, rows), jnp.float32)], axis=0).T
    query_high, query_low = high[...], low[...]
    query_all = jnp.concatenate([query_high, query_high, query_low], axis=1)
    dot = functools.partial(jnp.dot, preferred_element_type=jnp.float32)
    pair = 2 * BLOCK
    for start in range(0, columns, pair):
        parts = []
        for at in range(start, start + pair, BLOCK):
            b = at // BLOCK
            value = values[:, at : at + BLOCK]
            square = jnp.sum(value * value, axis=0, keepdims=True)
            for place in range(FAN):
                result[place, extra_at + b : extra_at + b + 1, :] = square
            parts.append(value * keep[:, b : b + 1])
        h, l = split(jnp.concatenate(parts, axis=1))
        product = dot(query_all, jnp.concatenate([h, l, h], axis=0))
        for place in range(FAN):
            for at in range(0, pair, BLOCK):
                b = (start + at) // BLOCK
                result[place, b * each : (b + 1) * each, :] = product[
                    place * each : (place + 1) * each, at : at + BLOCK
                ]


def local_gram(arrived, mask, events):
    rows, columns = events.shape
    shape = (FAN, QUERIES // FAN * (columns // BLOCK) + EXTRA, BLOCK)
    whole = pl.BlockSpec(memory_space=pltpu.VMEM)
    return pl.pallas_call(
        gram_kernel,
        in_specs=[whole, whole, whole],
        out_specs=whole,
        out_shape=jax.ShapeDtypeStruct(shape, jnp.float32),
        scratch_shapes=[
            pltpu.VMEM((QUERIES, rows), jnp.bfloat16),
            pltpu.VMEM((QUERIES, rows), jnp.bfloat16),
        ],
        compiler_params=pltpu.CompilerParams(vmem_limit_bytes=32 << 20),
        cost_estimate=pl.CostEstimate(
            flops=6 * QUERIES * rows * columns,
            bytes_accessed=4 * (rows * columns + QUERIES * columns),
            transcendentals=0,
        ),
        name="gram",
    )(arrived, mask, events)


def exchanged(parts, groups):
    return lax.all_to_all(
        parts, ALL, split_axis=0, concat_axis=0, tiled=True, axis_index_groups=groups
    )


def first_sum_kernel(arrived, total):
    rows = arrived.shape[1] - EXTRA
    each = QUERIES // FAN
    part = each // FAN

    def summed(at, size):
        whole = arrived[0, at : at + size, :]
        for sender in range(1, FAN):
            whole += arrived[sender, at : at + size, :]
        return whole

    for at in range(0, rows, each):
        whole = summed(at, each)
        for place in range(FAN):
            first = at // FAN
            total[place, first : first + part, :] = whole[place * part : (place + 1) * part]
    extra = summed(rows, EXTRA)
    for place in range(FAN):
        total[place, rows // FAN :, :] = extra


def first_sum(arrived):
    shape = (FAN, (arrived.shape[1] - EXTRA) // FAN + EXTRA, BLOCK)
    return pl.pallas_call(
        first_sum_kernel,
        out_shape=jax.ShapeDtypeStruct(shape, jnp.float32),
        compiler_params=pltpu.CompilerParams(vmem_limit_bytes=32 << 20),
        cost_estimate=pl.CostEstimate(
            flops=arrived.size, bytes_accessed=5 * arrived.size, transcendentals=0
        ),
        name="first_sum",
    )(arrived)


def second_sum_kernel(arrived, total, whole):
    rows = arrived.shape[1] - EXTRA
    value = arrived[0]
    for sender in range(1, FAN):
        value += arrived[sender]
    whole[...] = value
    each = QUERIES // (FAN * FAN)
    share = each // FAR
    blocks = rows // each
    for place in range(FAR):
        for query in range(share):
            for k in range(blocks // 2):
                first = place * share + query + 2 * k * each
                total[place, query * blocks // 2 + k] = whole[pl.ds(first, 2, stride=each), :]
        last = share * blocks // 2
        for k in range(total.shape[1] - last):
            total[place, last + k] = value[rows + 2 * k : rows + 2 * k + 2]


def second_sum(arrived):
    rows = arrived.shape[1] - EXTRA
    sums = rows * FAN * FAN // QUERIES + QUERIES // BLOCK
    shape = (FAR, (rows // FAR + sums) // 2, 2, BLOCK)
    return pl.pallas_call(
        second_sum_kernel,
        out_shape=jax.ShapeDtypeStruct(shape, jnp.float32),
        scratch_shapes=[pltpu.VMEM(arrived.shape[1:], jnp.float32)],
        compiler_params=pltpu.CompilerParams(vmem_limit_bytes=32 << 20),
        cost_estimate=pl.CostEstimate(
            flops=arrived.size, bytes_accessed=5 * arrived.size, transcendentals=0
        ),
        name="second_sum",
    )(arrived)


def last_sum_kernel(factor, arrived, queries, rates, similarity):
    total = arrived[0]
    for sender in range(1, FAR):
        total += arrived[sender]
    share, columns = similarity.shape
    half = columns // BLOCK // 2
    squares = total[share * half : (share + 1) * half]
    paired = jnp.stack([rates[2 * k : 2 * k + 2, :] for k in range(half)])
    weight = lax.rsqrt(squares * paired + EPSILON) * factor

    z, x, y = (lax.axis_index(a) for a in ROWS)
    mine = ((x * FAN + y * 2 + z % 2) * FAR + z // 2) * share
    group = z // (DEPTH // GROUPS)
    query_squares = total[(share + 1) * half]
    row = lax.broadcasted_iota(jnp.int32, query_squares.shape, 0)
    lane = lax.broadcasted_iota(jnp.int32, query_squares.shape, 1)
    at = QUERY_GROUP + 1
    query_rate = queries[0, at : at + 1, :1]
    for k in range(1, GROUPS):
        query_rate = jnp.where(group == k, queries[k, at : at + 1, :1], query_rate)
    for query in range(share):
        found = jnp.where(row * BLOCK + lane == mine + query, query_squares, 0.0)
        found = jnp.sum(jnp.sum(found, axis=1, keepdims=True), axis=0, keepdims=True)
        scale = lax.rsqrt(found * query_rate + EPSILON)
        result = total[query * half : (query + 1) * half] * weight * scale[None]
        for b in range(2 * half):
            similarity[query : query + 1, b * BLOCK : (b + 1) * BLOCK] = result[
                b // 2, b % 2 : b % 2 + 1
            ]


def last_sum(factor, arrived, queries, rates):
    shape = (QUERIES // (FAN * FAN * FAR), rates.shape[0] * BLOCK)
    return pl.pallas_call(
        functools.partial(last_sum_kernel, factor),
        out_shape=jax.ShapeDtypeStruct(shape, jnp.float32),
        compiler_params=pltpu.CompilerParams(vmem_limit_bytes=32 << 20),
        cost_estimate=pl.CostEstimate(
            flops=arrived.size, bytes_accessed=5 * arrived.size, transcendentals=0
        ),
        name="last_sum",
    )(arrived, queries, rates)


def shards(events, sample_mask, keep_rate):
    first, second, third = stages()
    mask = sample_mask.T
    arrived = lax.all_gather(own_queries(mask, events, keep_rate[None]), "cols")
    total = first_sum(exchanged(local_gram(arrived, mask, events), first))
    total = second_sum(exchanged(total, second))
    factor = math.sqrt(events.shape[0] * DEPTH * WIDTH * PAIR)
    rates = jnp.broadcast_to(keep_rate[:, None], (keep_rate.size, BLOCK))
    return last_sum(factor, exchanged(total, third), arrived, rates)


def solution(mesh):
    torus = Mesh(mesh.devices.reshape(DEPTH, WIDTH, PAIR, GROUPS), ALL)
    return jax.shard_map(
        shards,
        mesh=torus,
        in_specs=(P(ROWS, "cols"), P(ROWS, "cols"), P("cols")),
        out_specs=P(ROWS, "cols"),
        check_vma=False,
    )
```

```python
import functools
import math

import jax
import jax.numpy as jnp
from jax import lax
from jax.experimental import pallas as pl
from jax.experimental.pallas import tpu as pltpu
from jax.sharding import Mesh
from jax.sharding import PartitionSpec as P

QUERY_GROUP = 64
BLOCK = 128
ROWS = ("z", "x", "y")
ALL = ("z", "x", "y", "cols")
DEPTH, WIDTH, PAIR, GROUPS = 16, 4, 2, 4
FAN = 4
FAR = DEPTH // 2
QUERIES = GROUPS * QUERY_GROUP
EXTRA = 40
EPSILON = 1e-06


def device(z, x, y, c):
    return ((z * WIDTH + x) * PAIR + y) * GROUPS + c


def along_x():
    return {
        c: [
            [device(z, x, y, c) for x in range(WIDTH)]
            for z in range(DEPTH)
            for y in range(PAIR)
        ]
        for c in range(GROUPS)
    }


def along_pairs():
    return {
        c: [
            [device(2 * far + odd, x, y, c) for y in range(PAIR) for odd in range(2)]
            for far in range(FAR)
            for x in range(WIDTH)
        ]
        for c in range(GROUPS)
    }


def stages():
    x, pairs = along_x(), along_pairs()
    first = [g for c in range(GROUPS) for g in (pairs if c % 2 else x)[c]]
    second = [g for c in range(GROUPS) for g in (x if c % 2 else pairs)[c]]
    third = [
        [device(2 * far + odd, x, y, c) for far in range(FAR)]
        for odd in range(2)
        for x in range(WIDTH)
        for y in range(PAIR)
        for c in range(GROUPS)
    ]
    return first, second, third


def split(values):
    high = values.astype(jnp.bfloat16)
    low = (values - high.astype(jnp.float32)).astype(jnp.bfloat16)
    return high, low


def turned(left, right):
    return lax.dot_general(
        left,
        right,
        (((1,), (1,)), ((), ())),
        precision=lax.Precision.HIGHEST,
        preferred_element_type=jnp.float32,
    )


def query_kernel(mask, events, rate, sent, keeps, near, rates, come):
    copies = (
        pltpu.make_async_copy(events.at[:, pl.ds(0, BLOCK)], near, come.at[0]),
        pltpu.make_async_copy(mask.at[pl.ds(0, 8)], keeps, come.at[1]),
        pltpu.make_async_copy(rate, rates, come.at[2]),
    )
    for copy in copies:
        copy.start()
    rows = near.shape[0]
    n = lax.broadcasted_iota(jnp.int32, (QUERY_GROUP, BLOCK), 0)
    column = lax.broadcasted_iota(jnp.int32, (QUERY_GROUP, BLOCK), 1)
    x, y, low, next_, query = n >> 4, (n >> 3) & 1, (n >> 2) & 1, (n >> 1) & 1, n & 1
    source = (next_ * 2 + low) * 16 + x * 4 + y * 2 + query
    pick = (column == source).astype(jnp.float32).astype(jnp.bfloat16)
    for copy in copies:
        copy.wait()
    rest, total = near[...], None
    for _ in range(3):
        part = rest.astype(jnp.bfloat16)
        rest = rest - part.astype(jnp.float32)
        chosen = lax.dot_general(
            pick, part, (((1,), (1,)), ((), ())), preferred_element_type=jnp.float32
        )
        total = chosen if total is None else total + chosen
    sent[:QUERY_GROUP, :] = total
    keep = keeps[:1, :].astype(jnp.float32)
    scale = jnp.broadcast_to(rates[:, :1], (1, rows))
    sent[QUERY_GROUP:, :] = jnp.concatenate(
        [keep, scale, jnp.zeros((6, rows), jnp.float32)], axis=0
    )


def own_queries(mask, events, rate):
    rows = events.shape[0]
    there = pl.BlockSpec(memory_space=pl.ANY)
    return pl.pallas_call(
        query_kernel,
        in_specs=[there] * 3,
        out_shape=jax.ShapeDtypeStruct((QUERY_GROUP + 8, rows), jnp.float32),
        scratch_shapes=[
            pltpu.VMEM((8, rows), mask.dtype),
            pltpu.VMEM((rows, BLOCK), events.dtype),
            pltpu.VMEM(rate.shape, rate.dtype),
            pltpu.SemaphoreType.DMA((3,)),
        ],
        compiler_params=pltpu.CompilerParams(vmem_limit_bytes=56 << 20),
        cost_estimate=pl.CostEstimate(flops=1 << 24, bytes_accessed=1 << 18, transcendentals=0),
        name="queries",
    )(mask, events, rate)


def gram_kernel(arrived, mask, values, result, high, low):
    rows, columns = values.shape
    blocks = columns // BLOCK
    each = QUERIES // FAN
    extra_at = each * blocks
    run = QUERY_GROUP // (FAN * FAN)

    core = lax.axis_index("cols") % 2
    raw = []
    for place in range(FAN * FAN):
        parts, keeps = [], []
        for group in range(GROUPS):
            parts.append(arrived[group, place * run : (place + 1) * run, :])
            keep = arrived[group, QUERY_GROUP : QUERY_GROUP + 1, :]
            keeps.append(jnp.broadcast_to(keep, (run, rows)))
        raw.append(jnp.concatenate(parts, axis=0))
        h, l = split(raw[-1] * jnp.concatenate(keeps, axis=0))
        at = jnp.where(core == 0, place, place % FAN * FAN + place // FAN)
        at = pl.multiple_of(at * (run * GROUPS), run * GROUPS)
        high[pl.ds(at, run * GROUPS), :] = h
        low[pl.ds(at, run * GROUPS), :] = l
    raw = jnp.concatenate(raw, axis=0)
    sums = turned(jnp.ones((8, rows), jnp.float32), raw * raw)[:1]
    last = [sums[:, k : k + BLOCK] for k in range(0, QUERIES, BLOCK)]
    last.append(jnp.zeros((EXTRA - blocks - len(last), BLOCK), jnp.float32))
    last = jnp.concatenate(last, axis=0)
    for place in range(FAN):
        result[place, extra_at + blocks :, :] = last

    keep = mask[...].astype(jnp.float32)
    keep = jnp.concatenate([keep, jnp.zeros((BLOCK - blocks, rows), jnp.float32)], axis=0).T
    query_high, query_low = high[...], low[...]
    query_all = jnp.concatenate([query_high, query_high, query_low], axis=1)
    dot = functools.partial(jnp.dot, preferred_element_type=jnp.float32)
    pair = 2 * BLOCK
    for start in range(0, columns, pair):
        parts = []
        for at in range(start, start + pair, BLOCK):
            b = at // BLOCK
            value = values[:, at : at + BLOCK]
            square = jnp.sum(value * value, axis=0, keepdims=True)
            for place in range(FAN):
                result[place, extra_at + b : extra_at + b + 1, :] = square
            parts.append(value * keep[:, b : b + 1])
        h, l = split(jnp.concatenate(parts, axis=1))
        product = dot(query_all, jnp.concatenate([h, l, h], axis=0))
        for place in range(FAN):
            for at in range(0, pair, BLOCK):
                b = (start + at) // BLOCK
                result[place, b * each : (b + 1) * each, :] = product[
                    place * each : (place + 1) * each, at : at + BLOCK
                ]


def local_gram(arrived, mask, events):
    rows, columns = events.shape
    shape = (FAN, QUERIES // FAN * (columns // BLOCK) + EXTRA, BLOCK)
    whole = pl.BlockSpec(memory_space=pltpu.VMEM)
    return pl.pallas_call(
        gram_kernel,
        in_specs=[whole, whole, whole],
        out_specs=whole,
        out_shape=jax.ShapeDtypeStruct(shape, jnp.float32),
        scratch_shapes=[
            pltpu.VMEM((QUERIES, rows), jnp.bfloat16),
            pltpu.VMEM((QUERIES, rows), jnp.bfloat16),
        ],
        compiler_params=pltpu.CompilerParams(vmem_limit_bytes=32 << 20),
        cost_estimate=pl.CostEstimate(
            flops=6 * QUERIES * rows * columns,
            bytes_accessed=4 * (rows * columns + QUERIES * columns),
            transcendentals=0,
        ),
        name="gram",
    )(arrived, mask, events)


def exchanged(parts, groups):
    return lax.all_to_all(
        parts, ALL, split_axis=0, concat_axis=0, tiled=True, axis_index_groups=groups
    )


def first_sum_kernel(arrived, total):
    rows = arrived.shape[1] - EXTRA
    each = QUERIES // FAN
    part = each // FAN

    def summed(at, size):
        whole = arrived[0, at : at + size, :]
        for sender in range(1, FAN):
            whole += arrived[sender, at : at + size, :]
        return whole

    for at in range(0, rows, each):
        whole = summed(at, each)
        for place in range(FAN):
            first = at // FAN
            total[place, first : first + part, :] = whole[place * part : (place + 1) * part]
    extra = summed(rows, EXTRA)
    for place in range(FAN):
        total[place, rows // FAN :, :] = extra


def first_sum(arrived):
    shape = (FAN, (arrived.shape[1] - EXTRA) // FAN + EXTRA, BLOCK)
    return pl.pallas_call(
        first_sum_kernel,
        out_shape=jax.ShapeDtypeStruct(shape, jnp.float32),
        compiler_params=pltpu.CompilerParams(vmem_limit_bytes=32 << 20),
        cost_estimate=pl.CostEstimate(
            flops=arrived.size, bytes_accessed=5 * arrived.size, transcendentals=0
        ),
        name="first_sum",
    )(arrived)


def second_sum_kernel(arrived, total, whole):
    rows = arrived.shape[1] - EXTRA
    value = arrived[0]
    for sender in range(1, FAN):
        value += arrived[sender]
    whole[...] = value
    each = QUERIES // (FAN * FAN)
    share = each // FAR
    blocks = rows // each
    for place in range(FAR):
        for query in range(share):
            for k in range(blocks // 2):
                first = place * share + query + 2 * k * each
                total[place, query * blocks // 2 + k] = whole[pl.ds(first, 2, stride=each), :]
        last = share * blocks // 2
        for k in range(total.shape[1] - last):
            total[place, last + k] = value[rows + 2 * k : rows + 2 * k + 2]


def second_sum(arrived):
    rows = arrived.shape[1] - EXTRA
    sums = rows * FAN * FAN // QUERIES + QUERIES // BLOCK
    shape = (FAR, (rows // FAR + sums) // 2, 2, BLOCK)
    return pl.pallas_call(
        second_sum_kernel,
        out_shape=jax.ShapeDtypeStruct(shape, jnp.float32),
        scratch_shapes=[pltpu.VMEM(arrived.shape[1:], jnp.float32)],
        compiler_params=pltpu.CompilerParams(vmem_limit_bytes=32 << 20),
        cost_estimate=pl.CostEstimate(
            flops=arrived.size, bytes_accessed=5 * arrived.size, transcendentals=0
        ),
        name="second_sum",
    )(arrived)


def last_sum_kernel(factor, arrived, queries, rates, similarity):
    total = arrived[0]
    for sender in range(1, FAR):
        total += arrived[sender]
    share, columns = similarity.shape
    half = columns // BLOCK // 2
    squares = total[share * half : (share + 1) * half]
    paired = jnp.stack([rates[2 * k : 2 * k + 2, :] for k in range(half)])
    weight = lax.rsqrt(squares * paired + EPSILON) * factor

    z, x, y = (lax.axis_index(a) for a in ROWS)
    mine = ((x * FAN + y * 2 + z % 2) * FAR + z // 2) * share
    group = z // (DEPTH // GROUPS)
    query_squares = total[(share + 1) * half]
    row = lax.broadcasted_iota(jnp.int32, query_squares.shape, 0)
    lane = lax.broadcasted_iota(jnp.int32, query_squares.shape, 1)
    at = QUERY_GROUP + 1
    query_rate = queries[0, at : at + 1, :1]
    for k in range(1, GROUPS):
        query_rate = jnp.where(group == k, queries[k, at : at + 1, :1], query_rate)
    for query in range(share):
        found = jnp.where(row * BLOCK + lane == mine + query, query_squares, 0.0)
        found = jnp.sum(jnp.sum(found, axis=1, keepdims=True), axis=0, keepdims=True)
        scale = lax.rsqrt(found * query_rate + EPSILON)
        result = total[query * half : (query + 1) * half] * weight * scale[None]
        for b in range(2 * half):
            similarity[query : query + 1, b * BLOCK : (b + 1) * BLOCK] = result[
                b // 2, b % 2 : b % 2 + 1
            ]


def last_sum(factor, arrived, queries, rates):
    shape = (QUERIES // (FAN * FAN * FAR), rates.shape[0] * BLOCK)
    return pl.pallas_call(
        functools.partial(last_sum_kernel, factor),
        out_shape=jax.ShapeDtypeStruct(shape, jnp.float32),
        compiler_params=pltpu.CompilerParams(vmem_limit_bytes=32 << 20),
        cost_estimate=pl.CostEstimate(
            flops=arrived.size, bytes_accessed=5 * arrived.size, transcendentals=0
        ),
        name="last_sum",
    )(arrived, queries, rates)


def shards(events, sample_mask, keep_rate):
    first, second, third = stages()
    mask = sample_mask.T
    arrived = lax.all_gather(own_queries(mask, events, keep_rate[None]), "cols")
    total = first_sum(exchanged(local_gram(arrived, mask, events), first))
    total = second_sum(exchanged(total, second))
    factor = math.sqrt(events.shape[0] * DEPTH * WIDTH * PAIR)
    rates = jnp.broadcast_to(keep_rate[:, None], (keep_rate.size, BLOCK))
    return last_sum(factor, exchanged(total, third), arrived, rates)


def solution(mesh):
    torus = Mesh(mesh.devices.reshape(DEPTH, WIDTH, PAIR, GROUPS), ALL)
    return jax.shard_map(
        shards,
        mesh=torus,
        in_specs=(P(ROWS, "cols"), P(ROWS, "cols"), P("cols")),
        out_specs=P(ROWS, "cols"),
        check_vma=False,
    )
```

```python
import functools
import math

import jax
import jax.numpy as jnp
from jax import lax
from jax.experimental import pallas as pl
from jax.experimental.pallas import tpu as pltpu
from jax.sharding import Mesh
from jax.sharding import PartitionSpec as P

QUERY_GROUP = 64
BLOCK = 128
ROWS = ("z", "x", "y")
ALL = ("z", "x", "y", "cols")
DEPTH, WIDTH, PAIR, GROUPS = 16, 4, 2, 4
FAN = 4
FAR = DEPTH // 2
QUERIES = GROUPS * QUERY_GROUP
EXTRA = 40
EPSILON = 1e-06


def device(z, x, y, c):
    return ((z * WIDTH + x) * PAIR + y) * GROUPS + c


def along_x():
    return {
        c: [
            [device(z, x, y, c) for x in range(WIDTH)]
            for z in range(DEPTH)
            for y in range(PAIR)
        ]
        for c in range(GROUPS)
    }


def along_pairs():
    return {
        c: [
            [device(2 * far + odd, x, y, c) for y in range(PAIR) for odd in range(2)]
            for far in range(FAR)
            for x in range(WIDTH)
        ]
        for c in range(GROUPS)
    }


def stages():
    x, pairs = along_x(), along_pairs()
    first = [g for c in range(GROUPS) for g in (pairs if c % 2 else x)[c]]
    second = [g for c in range(GROUPS) for g in (x if c % 2 else pairs)[c]]
    third = [
        [device(2 * far + odd, x, y, c) for far in range(FAR)]
        for odd in range(2)
        for x in range(WIDTH)
        for y in range(PAIR)
        for c in range(GROUPS)
    ]
    return first, second, third


def split(values):
    high = values.astype(jnp.bfloat16)
    low = (values - high.astype(jnp.float32)).astype(jnp.bfloat16)
    return high, low


def query_kernel(mask, events, rate, sent, keeps, near, rates, come):
    copies = (
        pltpu.make_async_copy(events.at[:, pl.ds(0, BLOCK)], near, come.at[0]),
        pltpu.make_async_copy(mask.at[pl.ds(0, 8)], keeps, come.at[1]),
        pltpu.make_async_copy(rate, rates, come.at[2]),
    )
    for copy in copies:
        copy.start()
    rows = near.shape[0]
    n = lax.broadcasted_iota(jnp.int32, (QUERY_GROUP, BLOCK), 0)
    column = lax.broadcasted_iota(jnp.int32, (QUERY_GROUP, BLOCK), 1)
    x, y, low, next_, query = n >> 4, (n >> 3) & 1, (n >> 2) & 1, (n >> 1) & 1, n & 1
    source = (next_ * 2 + low) * 16 + x * 4 + y * 2 + query
    pick = (column == source).astype(jnp.float32).astype(jnp.bfloat16)
    for copy in copies:
        copy.wait()
    rest, total = near[...], None
    for _ in range(3):
        part = rest.astype(jnp.bfloat16)
        rest = rest - part.astype(jnp.float32)
        chosen = lax.dot_general(
            pick, part, (((1,), (1,)), ((), ())), preferred_element_type=jnp.float32
        )
        total = chosen if total is None else total + chosen
    sent[:QUERY_GROUP, :] = total
    keep = keeps[:1, :].astype(jnp.float32)
    scale = jnp.broadcast_to(rates[:, :1], (1, rows))
    sent[QUERY_GROUP:, :] = jnp.concatenate(
        [keep, scale, jnp.zeros((6, rows), jnp.float32)], axis=0
    )


def own_queries(mask, events, rate):
    rows = events.shape[0]
    there = pl.BlockSpec(memory_space=pl.ANY)
    return pl.pallas_call(
        query_kernel,
        in_specs=[there] * 3,
        out_shape=jax.ShapeDtypeStruct((QUERY_GROUP + 8, rows), jnp.float32),
        scratch_shapes=[
            pltpu.VMEM((8, rows), mask.dtype),
            pltpu.VMEM((rows, BLOCK), events.dtype),
            pltpu.VMEM(rate.shape, rate.dtype),
            pltpu.SemaphoreType.DMA((3,)),
        ],
        compiler_params=pltpu.CompilerParams(vmem_limit_bytes=56 << 20),
        cost_estimate=pl.CostEstimate(flops=1 << 24, bytes_accessed=1 << 18, transcendentals=0),
        name="queries",
    )(mask, events, rate)


def gram_kernel(arrived, mask, values, result, high, low):
    rows, columns = values.shape
    blocks = columns // BLOCK
    each = QUERIES // FAN
    extra_at = each * blocks
    run = QUERY_GROUP // (FAN * FAN)

    core = lax.axis_index("cols") % 2
    raw = []
    for place in range(FAN * FAN):
        parts, keeps = [], []
        for group in range(GROUPS):
            parts.append(arrived[group, place * run : (place + 1) * run, :])
            keep = arrived[group, QUERY_GROUP : QUERY_GROUP + 1, :]
            keeps.append(jnp.broadcast_to(keep, (run, rows)))
        raw.append(jnp.concatenate(parts, axis=0))
        h, l = split(raw[-1] * jnp.concatenate(keeps, axis=0))
        at = jnp.where(core == 0, place, place % FAN * FAN + place // FAN)
        at = pl.multiple_of(at * (run * GROUPS), run * GROUPS)
        high[pl.ds(at, run * GROUPS), :] = h
        low[pl.ds(at, run * GROUPS), :] = l
    raw = jnp.concatenate(raw, axis=0)
    rest, sums = raw * raw, None
    for _ in range(3):
        part = rest.astype(jnp.bfloat16)
        rest = rest - part.astype(jnp.float32)
        added = lax.dot_general(
            jnp.ones((8, rows), jnp.bfloat16),
            part,
            (((1,), (1,)), ((), ())),
            preferred_element_type=jnp.float32,
        )[:1]
        sums = added if sums is None else sums + added
    last = [sums[:, k : k + BLOCK] for k in range(0, QUERIES, BLOCK)]
    last.append(jnp.zeros((EXTRA - blocks - len(last), BLOCK), jnp.float32))
    last = jnp.concatenate(last, axis=0)
    for place in range(FAN):
        result[place, extra_at + blocks :, :] = last

    keep = mask[...].astype(jnp.float32)
    keep = jnp.concatenate([keep, jnp.zeros((BLOCK - blocks, rows), jnp.float32)], axis=0).T
    query_high, query_low = high[...], low[...]
    query_all = jnp.concatenate([query_high, query_high, query_low], axis=1)
    dot = functools.partial(jnp.dot, preferred_element_type=jnp.float32)
    pair = 2 * BLOCK
    for start in range(0, columns, pair):
        parts = []
        for at in range(start, start + pair, BLOCK):
            b = at // BLOCK
            value = values[:, at : at + BLOCK]
            square = jnp.sum(value * value, axis=0, keepdims=True)
            for place in range(FAN):
                result[place, extra_at + b : extra_at + b + 1, :] = square
            parts.append(value * keep[:, b : b + 1])
        h, l = split(jnp.concatenate(parts, axis=1))
        product = dot(query_all, jnp.concatenate([h, l, h], axis=0))
        for place in range(FAN):
            for at in range(0, pair, BLOCK):
                b = (start + at) // BLOCK
                result[place, b * each : (b + 1) * each, :] = product[
                    place * each : (place + 1) * each, at : at + BLOCK
                ]


def local_gram(arrived, mask, events):
    rows, columns = events.shape
    shape = (FAN, QUERIES // FAN * (columns // BLOCK) + EXTRA, BLOCK)
    whole = pl.BlockSpec(memory_space=pltpu.VMEM)
    return pl.pallas_call(
        gram_kernel,
        in_specs=[whole, whole, whole],
        out_specs=whole,
        out_shape=jax.ShapeDtypeStruct(shape, jnp.float32),
        scratch_shapes=[
            pltpu.VMEM((QUERIES, rows), jnp.bfloat16),
            pltpu.VMEM((QUERIES, rows), jnp.bfloat16),
        ],
        compiler_params=pltpu.CompilerParams(vmem_limit_bytes=32 << 20),
        cost_estimate=pl.CostEstimate(
            flops=6 * QUERIES * rows * columns,
            bytes_accessed=4 * (rows * columns + QUERIES * columns),
            transcendentals=0,
        ),
        name="gram",
    )(arrived, mask, events)


def exchanged(parts, groups):
    return lax.all_to_all(
        parts, ALL, split_axis=0, concat_axis=0, tiled=True, axis_index_groups=groups
    )


def first_sum_kernel(arrived, total):
    rows = arrived.shape[1] - EXTRA
    each = QUERIES // FAN
    part = each // FAN

    def summed(at, size):
        whole = arrived[0, at : at + size, :]
        for sender in range(1, FAN):
            whole += arrived[sender, at : at + size, :]
        return whole

    for at in range(0, rows, each):
        whole = summed(at, each)
        for place in range(FAN):
            first = at // FAN
            total[place, first : first + part, :] = whole[place * part : (place + 1) * part]
    extra = summed(rows, EXTRA)
    for place in range(FAN):
        total[place, rows // FAN :, :] = extra


def first_sum(arrived):
    shape = (FAN, (arrived.shape[1] - EXTRA) // FAN + EXTRA, BLOCK)
    return pl.pallas_call(
        first_sum_kernel,
        out_shape=jax.ShapeDtypeStruct(shape, jnp.float32),
        compiler_params=pltpu.CompilerParams(vmem_limit_bytes=32 << 20),
        cost_estimate=pl.CostEstimate(
            flops=arrived.size, bytes_accessed=5 * arrived.size, transcendentals=0
        ),
        name="first_sum",
    )(arrived)


def second_sum_kernel(arrived, total, whole):
    rows = arrived.shape[1] - EXTRA
    value = arrived[0]
    for sender in range(1, FAN):
        value += arrived[sender]
    whole[...] = value
    each = QUERIES // (FAN * FAN)
    share = each // FAR
    blocks = rows // each
    for place in range(FAR):
        for query in range(share):
            for k in range(blocks // 2):
                first = place * share + query + 2 * k * each
                total[place, query * blocks // 2 + k] = whole[pl.ds(first, 2, stride=each), :]
        last = share * blocks // 2
        for k in range(total.shape[1] - last):
            total[place, last + k] = value[rows + 2 * k : rows + 2 * k + 2]


def second_sum(arrived):
    rows = arrived.shape[1] - EXTRA
    sums = rows * FAN * FAN // QUERIES + QUERIES // BLOCK
    shape = (FAR, (rows // FAR + sums) // 2, 2, BLOCK)
    return pl.pallas_call(
        second_sum_kernel,
        out_shape=jax.ShapeDtypeStruct(shape, jnp.float32),
        scratch_shapes=[pltpu.VMEM(arrived.shape[1:], jnp.float32)],
        compiler_params=pltpu.CompilerParams(vmem_limit_bytes=32 << 20),
        cost_estimate=pl.CostEstimate(
            flops=arrived.size, bytes_accessed=5 * arrived.size, transcendentals=0
        ),
        name="second_sum",
    )(arrived)


def last_sum_kernel(factor, arrived, queries, rates, similarity):
    total = arrived[0]
    for sender in range(1, FAR):
        total += arrived[sender]
    share, columns = similarity.shape
    half = columns // BLOCK // 2
    squares = total[share * half : (share + 1) * half]
    paired = jnp.stack([rates[2 * k : 2 * k + 2, :] for k in range(half)])
    weight = lax.rsqrt(squares * paired + EPSILON) * factor

    z, x, y = (lax.axis_index(a) for a in ROWS)
    mine = ((x * FAN + y * 2 + z % 2) * FAR + z // 2) * share
    group = z // (DEPTH // GROUPS)
    query_squares = total[(share + 1) * half]
    row = lax.broadcasted_iota(jnp.int32, query_squares.shape, 0)
    lane = lax.broadcasted_iota(jnp.int32, query_squares.shape, 1)
    at = QUERY_GROUP + 1
    query_rate = queries[0, at : at + 1, :1]
    for k in range(1, GROUPS):
        query_rate = jnp.where(group == k, queries[k, at : at + 1, :1], query_rate)
    for query in range(share):
        found = jnp.where(row * BLOCK + lane == mine + query, query_squares, 0.0)
        found = jnp.sum(jnp.sum(found, axis=1, keepdims=True), axis=0, keepdims=True)
        scale = lax.rsqrt(found * query_rate + EPSILON)
        result = total[query * half : (query + 1) * half] * weight * scale[None]
        for b in range(2 * half):
            similarity[query : query + 1, b * BLOCK : (b + 1) * BLOCK] = result[
                b // 2, b % 2 : b % 2 + 1
            ]


def last_sum(factor, arrived, queries, rates):
    shape = (QUERIES // (FAN * FAN * FAR), rates.shape[0] * BLOCK)
    return pl.pallas_call(
        functools.partial(last_sum_kernel, factor),
        out_shape=jax.ShapeDtypeStruct(shape, jnp.float32),
        compiler_params=pltpu.CompilerParams(vmem_limit_bytes=32 << 20),
        cost_estimate=pl.CostEstimate(
            flops=arrived.size, bytes_accessed=5 * arrived.size, transcendentals=0
        ),
        name="last_sum",
    )(arrived, queries, rates)


def shards(events, sample_mask, keep_rate):
    first, second, third = stages()
    mask = sample_mask.T
    arrived = lax.all_gather(own_queries(mask, events, keep_rate[None]), "cols")
    total = first_sum(exchanged(local_gram(arrived, mask, events), first))
    total = second_sum(exchanged(total, second))
    factor = math.sqrt(events.shape[0] * DEPTH * WIDTH * PAIR)
    rates = jnp.broadcast_to(keep_rate[:, None], (keep_rate.size, BLOCK))
    return last_sum(factor, exchanged(total, third), arrived, rates)


def solution(mesh):
    torus = Mesh(mesh.devices.reshape(DEPTH, WIDTH, PAIR, GROUPS), ALL)
    return jax.shard_map(
        shards,
        mesh=torus,
        in_specs=(P(ROWS, "cols"), P(ROWS, "cols"), P("cols")),
        out_specs=P(ROWS, "cols"),
        check_vma=False,
    )
```
